256 devices in a mesh: wide: 32 (over z, x), narrow: 8 (over y, core).
Axes of the slice: x: 4, y: 4, z: 8, core: 2. Of those that a mesh axis runs over, the one named last changes fastest.
Arguments:
- grid_adjoint_fields: bfloat16 [256, 2560, 512], P('wide', 'narrow'), may hold values from -6 to 6
- interp_weights: bfloat16 [20480, 32, 32], P(('wide', 'narrow')), may hold values from -1 to 1
- depart_owner: int32 [20480, 1], P(('wide', 'narrow')), may hold values from 0 to 31; in each aligned block of 80 rows (0 to 79, 80 to 159, ...) at most 5 rows name the same one
- depart_block: int32 [20480], P(('wide', 'narrow')), may hold values from 0 to 79
- wave_perm: int32 [512], replicated, may hold values from 0 to 511, each once
- legendre: bfloat16 [512, 256, 512], P(('wide', 'narrow')), may hold values from -0.375 to 0.375
- mode_proj: float32 [512, 512], replicated, may hold values from -0.25 to 0.25
- mode_back: float32 [512, 512], replicated, may hold values from -0.25 to 0.25
- mode_depth: float32 [512], replicated, may hold values from 1e-06 to 0.001
Outputs:
- adj_out: float32 [256, 2560, 512], P('wide', 'narrow')
The draws below stay inside these ranges and needn't reach their ends.
Inputs may be any that keep to these rules, and one draw needn't show every extreme that they name: `depart_owner`: each block's departure owner shares the block's narrow index. Among the 80 blocks of one device at most 5 name one owner, and exactly 5 do in some devices. `wave_perm`: every wavenumber appears once.
All inputs are finite; a program needn't handle non-finite values.
Results may differ from the reference program's by a relative error of at most 0.013.
Values may be sent and summed in bfloat16 or wider, within the bound.
No kernel may reach another device: no remote copies, remote signals or barrier semaphores. Data moves between devices by JAX's collectives and lax.ppermute only.
A program may use at most 256 MiB of HBM per device.

```python
import math
import jax
import jax.numpy as jnp
import numpy as np
from jax import lax

NLON = 2560
M = 512
LAT_DEV = 8
BS = 32
C = 512
NLAT = 256
LON_DEV = 320
NB_DEV = 80
NBLOCKS = 20480
CAP = 5
N_WIDE = 32
N_NARROW = 8


def plant(result, stream_key, low, top_value):
    place = [jax.random.randint(jax.random.fold_in(stream_key, axis), (), 0, length) for axis, length in enumerate(result.shape)]
    widest = result.shape.index(max(result.shape))
    neighbour = place[:widest] + [(place[widest] + 1) % result.shape[widest]] + place[widest + 1:]
    return result.at[tuple(place)].set(low).at[tuple(neighbour)].set(top_value)


def shard_levels(stream_key, shape, cuts, low, top_value):
    factor_of, own = 1.0, jax.random.fold_in(stream_key, 6)
    for position, blocks in cuts:
        draws = jnp.exp(jax.random.uniform(jax.random.fold_in(own, position), (blocks,), jnp.float32, low / len(cuts), top_value / len(cuts)))
        factor_of = factor_of * jnp.repeat(draws, shape[position] // blocks).reshape([-1 if axis == position else 1 for axis in range(len(shape))])
    return factor_of


def deal_out(key, own, number, rows, count, top, limit, skew):
    order = jax.random.permutation(key, count)
    crowded, common = portions_of(count, rows * top, limit, skew, True), portions_of(count, rows * top, limit, skew, False)
    places = jnp.arange(count)

    def named(lengths, rotation):
        used = int((lengths > 0).sum())
        fixed = max(1, used // 4)
        shifted = fixed + (places - fixed + rotation * (used - fixed)) % max(1, count - fixed)
        return jnp.zeros((count,), jnp.int32).at[order[jnp.where(places < fixed, places, shifted)]].set(jnp.asarray(lengths, jnp.int32))

    lengths = jnp.where(number % 4 == 0, named(crowded, number // 4), named(common, number - number // 4 - 1))
    mixed = jax.random.permutation(jax.random.fold_in(own, 3), count)
    donor, taker = mixed[0:count // 2 * 2:2], mixed[1:count // 2 * 2:2]
    room = jnp.minimum(lengths[donor] - 1, limit - lengths[taker]) // 2
    room = jnp.where((donor == order[0]) | (taker == order[0]) | (lengths[taker] == 0), 0, jnp.maximum(room, 0))
    shifted = jax.random.randint(jax.random.fold_in(own, 4), (count // 2,), 0, 1 << 20) % (room + 1)
    lengths = lengths.at[donor].add(-shifted).at[taker].add(shifted)
    members = jnp.searchsorted(jnp.cumsum(lengths), jnp.arange(rows * top), side="right").astype(jnp.int32)
    grid = members.reshape(top, rows).T
    grid = grid[jax.random.permutation(jax.random.fold_in(own, 1), rows)]
    rotation = jax.random.randint(jax.random.fold_in(own, 2), (rows, 1), 0, top)
    return jnp.take_along_axis(grid, (jnp.arange(top)[None, :] + rotation) % top, axis=1)


def portions_of(amount, total, most, skew, full):
    portions = [(1 << 20) // math.isqrt(rank ** skew) + 1 for rank in range(1, amount + 1)]
    largest = most if full else min(most, max(-(-total // amount), total * portions[0] // sum(portions)))
    least = 1 if total - largest >= amount - 1 else 0
    holding, rest = [largest] + [least] * (amount - 1), total - largest - least * (amount - 1)
    while rest > 0:
        free = [i for i in range(1, amount) if holding[i] < largest] or [i for i in range(1, amount) if holding[i] < most]
        whole, budget = sum([portions[i] for i in free]), rest
        for i in free:
            more = min(most - holding[i], max(1, budget * portions[i] // whole), rest)
            holding[i] = holding[i] + more
            rest = rest - more
    return np.array(holding)


def centred(stream_key, extent, deviation, bound, cuts=(), kind=jnp.bfloat16):
    entries = deviation * jax.random.normal(stream_key, extent, jnp.float32)
    if cuts:
        entries = entries * shard_levels(stream_key, extent, cuts, -0.22, 0.18)
    return jnp.clip(entries, -bound, bound).astype(kind)


def setup_inputs(seed: int = 0) -> dict:
    streams_of = jax.random.split(jax.random.key(seed), 10)
    grid_adjoint_fields = centred(streams_of[0], (NLAT, NLON, C), 1.0, 6.0, ((0, 32), (1, 8)))
    interp_weights = centred(streams_of[1], (NBLOCKS, BS, BS), BS ** -0.5, 1.0, ((0, 256),))
    depart_owner_keys = jax.random.split(jax.random.fold_in(streams_of[2], 1), NBLOCKS // NB_DEV)
    depart_owner_turns = jax.random.permutation(jax.random.fold_in(streams_of[2], 3), NBLOCKS // NB_DEV)
    depart_owner = jax.vmap(lambda own, number: deal_out(jax.random.fold_in(streams_of[2], 2), own, number, NB_DEV, N_WIDE, 1, CAP, 2))(depart_owner_keys, depart_owner_turns).reshape((NBLOCKS, 1))
    depart_block = plant(jax.random.randint(streams_of[3], (NBLOCKS,), 0, NB_DEV), jax.random.fold_in(streams_of[3], 1), 0, NB_DEV - 1).astype(jnp.int32)
    wave_perm = jax.random.permutation(streams_of[4], M).astype(jnp.int32)
    legendre = centred(streams_of[5], (M, NLAT, M), NLAT ** -0.5, 0.375, ((0, 256),))
    mode_proj = centred(streams_of[6], (C, C), C ** -0.5, 0.25, (), jnp.float32)
    mode_back = centred(streams_of[7], (C, C), C ** -0.5, 0.25, (), jnp.float32)
    mode_depth = jnp.clip(jnp.exp(jax.random.uniform(streams_of[8], (C,), jnp.float32, math.log(9.999999974752427e-07), math.log(0.001))), 9.999999974752427e-07, 0.001)
    return dict(grid_adjoint_fields=grid_adjoint_fields, interp_weights=interp_weights, depart_owner=depart_owner, depart_block=depart_block, wave_perm=wave_perm, legendre=legendre, mode_proj=mode_proj, mode_back=mode_back, mode_depth=mode_depth)


def trig_table(lon_index, col_index, wave_perm):
    wavenumber = jnp.take(wave_perm, col_index // 2)
    phase_int = (lon_index[:, None] * wavenumber[None, :]) % NLON
    angles = phase_int.astype(jnp.float32) * (2.0 * math.pi / NLON)
    values = jnp.where((col_index % 2 == 0)[None, :], jnp.cos(angles), jnp.sin(angles))
    return values.astype(jnp.bfloat16)


def apply_modes(spectra, mode_proj, mode_back, mode_depth):
    slot_count, degrees, parts, channels = spectra.shape
    mode_rows = jnp.dot(spectra.reshape(-1, channels), mode_proj, precision=lax.Precision.HIGHEST, preferred_element_type=jnp.float32)
    degree_float = jnp.arange(degrees, dtype=jnp.float32)
    damping = 1.0 / (1.0 + (degree_float * (degree_float + 1.0))[:, None] * mode_depth[None, :])
    mode_rows = mode_rows.reshape(slot_count, degrees, parts, channels) * damping[None, :, None, :]
    returned = jnp.dot(mode_rows.reshape(-1, channels), mode_back, precision=lax.Precision.HIGHEST, preferred_element_type=jnp.float32)
    return returned.astype(jnp.bfloat16).reshape(slot_count, degrees, parts, channels)


def reference(grid_adjoint_fields, interp_weights, depart_owner, depart_block, wave_perm, legendre, mode_proj, mode_back, mode_depth):
    normalizing_scale = NLON ** -0.5
    trig_rows = trig_table(jnp.arange(NLON, dtype=jnp.int32), jnp.arange(2 * M, dtype=jnp.int32), wave_perm)
    trigonometric_floats = trig_rows.astype(jnp.float32)
    fourier_harmonics = (jnp.einsum('brw,rk->bkw', grid_adjoint_fields.astype(jnp.float32), trigonometric_floats) * normalizing_scale).astype(jnp.bfloat16)
    degree = jnp.arange(M, dtype=jnp.int32)
    keep_mask = degree[None, None, :] >= wave_perm[:, None, None]
    masked_values = jnp.where(keep_mask, legendre, jnp.zeros_like(legendre)).astype(jnp.float32)
    fourier_sets = fourier_harmonics.reshape(NLAT, M, 2, C).astype(jnp.float32)
    spectra = jnp.einsum('jgn,gjpc->jnpc', masked_values, fourier_sets)
    returned = apply_modes(spectra, mode_proj, mode_back, mode_depth)
    synthesis_output = jnp.einsum('jgn,jnpc->gjpc', masked_values, returned.astype(jnp.float32)).astype(jnp.bfloat16)
    synthesis_output = synthesis_output.reshape(NLAT, 2 * M, C)
    wavenumber_grid = (jnp.einsum('yzw,rz->yrw', synthesis_output.astype(jnp.float32), trigonometric_floats) * normalizing_scale).astype(jnp.bfloat16)
    blocks_per_row = LON_DEV // BS
    blocks = grid_adjoint_fields.reshape(N_WIDE, LAT_DEV, N_NARROW, blocks_per_row, BS, C).transpose(0, 2, 1, 3, 4, 5).reshape(NBLOCKS, BS, C)
    contrib = jnp.einsum('bai,bac->bic', interp_weights.astype(jnp.float32), blocks.astype(jnp.float32)).astype(jnp.bfloat16)
    source = jnp.arange(NBLOCKS, dtype=jnp.int32)
    narrow_of = (source // NB_DEV) % N_NARROW
    target = (depart_owner[:, 0] * N_NARROW + narrow_of) * NB_DEV + depart_block
    deposit = jax.ops.segment_sum(contrib.astype(jnp.float32), target, num_segments=NBLOCKS)
    deposit_grid = deposit.reshape(N_WIDE, N_NARROW, LAT_DEV, blocks_per_row, BS, C).transpose(0, 2, 1, 3, 4, 5).reshape(NLAT, NLON, C)
    return wavenumber_grid.astype(jnp.float32) + deposit_grid
```

```python
import math

import numpy as np
import jax
import jax.numpy as jnp
from jax import lax
from jax.experimental import pallas as pl
from jax.experimental.pallas import tpu as pltpu
from jax.sharding import PartitionSpec as P

NLON = 2560
BS = 32
CAP = 5
BF = jnp.bfloat16
F32 = jnp.float32


def _half_sine_coefficients():
    nodes = (np.cos(np.pi * (np.arange(64) + 0.5) / 64) + 1) * 0.5 * (np.pi / 2) ** 2
    root = np.sqrt(nodes)
    return [float(c) for c in np.polynomial.polynomial.polyfit(nodes, np.sin(root) / root, 5)]


SINE = _half_sine_coefficients()


def cosine_of_phase(phase):
    turns = jnp.round(phase * (1.0 / NLON))
    u = (phase - turns * NLON) * (math.pi / NLON)
    z = u * u
    poly = jnp.full_like(z, SINE[-1])
    for coefficient in SINE[-2::-1]:
        poly = poly * z + coefficient
    s = u * poly
    return (1.0 - 2.0 * s * s).astype(BF)


def dft_body(core_ref, t_ref, own_ref, got_ref, *outs):
    for lat in range(own_ref.shape[0]):
        x = jnp.concatenate([own_ref[lat], got_ref[lat]], axis=0)
        r = jnp.dot(t_ref[...], x, preferred_element_type=F32)
        for i, o in enumerate(outs):
            o[lat] = r[128 * i : 128 * i + 128].astype(BF)


def dft(core, table, x, got, step):
    rows = table.shape[0]
    lat, lon, channels = x.shape
    half = channels // 2
    n = rows // 128
    return pl.pallas_call(
        dft_body,
        out_shape=[jax.ShapeDtypeStruct((lat, 128, half), BF)] * n,
        grid_spec=pltpu.PrefetchScalarGridSpec(
            num_scalar_prefetch=1,
            grid=(lat // step,),
            in_specs=[
                pl.BlockSpec((rows, 2 * lon), lambda i, c: (0, 0)),
                pl.BlockSpec((step, lon, half), lambda i, c: (i, 0, c[0])),
                pl.BlockSpec((step, lon, half), lambda i, c: (i, 0, 0)),
            ],
            out_specs=[pl.BlockSpec((step, 128, half), lambda i, c: (i, 0, 0))] * n,
        ),
        compiler_params=pltpu.CompilerParams(vmem_limit_bytes=48 << 20),
        name="dft",
    )(core, table, x, got)


def rows_body(own_a, sum_a, direct_a, own_b, sum_b, direct_b, marks, o_ref, tmp):
    wide, lat, _ = o_ref.shape
    half = own_a.shape[2]
    for s, parts in enumerate(((own_a, sum_a, direct_a), (own_b, sum_b, direct_b))):
        for q in range(4):
            for h in range(half // 128):
                t = tmp.at[(q * (half // 128) + h) % 4]
                lanes = slice(128 * h, 128 * h + 128)
                for l in range(lat):
                    value = sum(p[l, wide * q : wide * q + wide, lanes].astype(F32) for p in parts)
                    value = value * NLON ** (-0.5)
                    for j in range(wide // 8):
                        t[pl.ds(lat * 8 * j + l, 8, stride=lat), :] = value[8 * j : 8 * j + 8]
                col = (s * 4 + q) * half + 128 * h
                o_ref[:, :, col : col + 128] = t[...].astype(BF).reshape(wide, lat, 128)
    o_ref[:, :, 8 * half :] = marks[...]


def to_rows(pieces, marks, wide):
    lat, _, half = pieces[0].shape
    return pl.pallas_call(
        rows_body,
        out_shape=jax.ShapeDtypeStruct((wide, lat, 8 * half + 128), BF),
        scratch_shapes=[pltpu.VMEM((4, wide * lat, 128), F32)],
        compiler_params=pltpu.CompilerParams(vmem_limit_bytes=48 << 20),
        name="to_rows",
    )(*pieces, marks)


def modes_body(f0_ref, f1_ref, mt_ref, m_ref, proj_ref, back_ref, damp_ref, o_ref):
    f = jnp.concatenate([f0_ref[...], f1_ref[...]], axis=1)
    spectra = jnp.dot(mt_ref[0], f, preferred_element_type=F32)
    modal = jnp.dot(spectra.astype(BF), proj_ref[...], preferred_element_type=F32) * damp_ref[...]
    back = jnp.dot(modal.astype(BF), back_ref[...], preferred_element_type=F32).astype(BF)
    synth = jnp.dot(m_ref[0], back, preferred_element_type=F32).astype(BF)
    wide, _, lat, half = o_ref.shape
    o_ref[:, 0] = synth[:, :half].reshape(wide, lat, half)
    o_ref[:, 1] = synth[:, half:].reshape(wide, lat, half)


def modes(f, other, masked_t, masked, proj, back, damp, wide, lat):
    total = f.shape[0]
    slots, degrees, _ = masked_t.shape
    channels = proj.shape[0]
    half = channels // 2
    return pl.pallas_call(
        modes_body,
        out_shape=jax.ShapeDtypeStruct((wide, 2, lat, 4 * half), BF),
        grid=(slots, 2),
        in_specs=[
            pl.BlockSpec((total, half), lambda k, p: (0, p * 2 + k)),
            pl.BlockSpec((total, half), lambda k, p: (0, p * 2 + k)),
            pl.BlockSpec((1, degrees, total), lambda k, p: (k, 0, 0)),
            pl.BlockSpec((1, total, degrees), lambda k, p: (k, 0, 0)),
            pl.BlockSpec((channels, channels), lambda k, p: (0, 0)),
            pl.BlockSpec((channels, channels), lambda k, p: (0, 0)),
            pl.BlockSpec((degrees, channels), lambda k, p: (0, 0)),
        ],
        out_specs=pl.BlockSpec((wide, 2, lat, half), lambda k, p: (0, 0, 0, p * 2 + k)),
        compiler_params=pltpu.CompilerParams(vmem_limit_bytes=48 << 20),
        name="modes",
    )(f, other, masked_t, masked, proj, back, damp)


def columns_body(keep, take, o_a, o_b, tmp):
    wide, lat, _ = take.shape
    half = o_a.shape[2]
    for s, (src, o) in enumerate(((keep, o_a), (take, o_b))):
        for q in range(4):
            for h in range(half // 128):
                t = tmp.at[(q * (half // 128) + h) % 4]
                col = slice(half * q + 128 * h, half * q + 128 * h + 128)
                value = src[:, 0, :, col] if s == 0 else src[:, :, col]
                t[...] = value.astype(F32).reshape(wide * lat, 128)
                for l in range(lat):
                    rows = [t[pl.ds(lat * 8 * j + l, 8, stride=lat), :] for j in range(wide // 8)]
                    rows = jnp.concatenate(rows, axis=0).astype(BF)
                    o[l, wide * q : wide * q + wide, 128 * h : 128 * h + 128] = rows


def to_columns(keep, take):
    wide, lat, width = take.shape
    half = width // 4
    return pl.pallas_call(
        columns_body,
        out_shape=[jax.ShapeDtypeStruct((lat, 4 * wide, half), BF)] * 2,
        grid=(1,),
        in_specs=[
            pl.BlockSpec((wide, 1, lat, width), lambda i: (0, 0, 0, 0)),
            pl.BlockSpec((wide, lat, width), lambda i: (0, 0, 0)),
        ],
        out_specs=[pl.BlockSpec((lat, 4 * wide, half), lambda i: (0, 0, 0))] * 2,
        scratch_shapes=[pltpu.VMEM((4, wide * lat, 128), F32)],
        compiler_params=pltpu.CompilerParams(vmem_limit_bytes=48 << 20),
        name="to_columns",
    )(keep, take)


def idft_body(t_ref, *refs):
    pieces, o_ref = refs[:8], refs[8]
    for lat in range(o_ref.shape[0]):
        g = jnp.concatenate([p[lat] for p in pieces], axis=0)
        r = jnp.dot(t_ref[...], g, preferred_element_type=F32)
        o_ref[lat] = (r * NLON ** (-0.5)).astype(BF)


def idft(table, pieces, step):
    lat, rows, half = pieces[0].shape
    lon = table.shape[0]
    return pl.pallas_call(
        idft_body,
        out_shape=jax.ShapeDtypeStruct((lat, lon, half), BF),
        grid=(lat // step,),
        in_specs=[pl.BlockSpec(table.shape, lambda i: (0, 0))]
        + [pl.BlockSpec((step, rows, half), lambda i: (i, 0, 0))] * 8,
        out_specs=pl.BlockSpec((step, lon, half), lambda i: (i, 0, 0)),
        compiler_params=pltpu.CompilerParams(vmem_limit_bytes=48 << 20),
        name="idft",
    )(table, *pieces)


def pack_body(slot_ref, contrib_ref, *outs):
    blocks = contrib_ref.shape[0]
    rows = contrib_ref.shape[1] // len(outs)

    def step(b, _):
        s = slot_ref[b]
        for i, o in enumerate(outs):
            o[s] = contrib_ref[b, pl.ds(i * rows, rows), :]
        return 0

    lax.fori_loop(0, blocks, step, 0)


def pack(slot, contrib, slots, parts):
    blocks, rows, channels = contrib.shape
    return pl.pallas_call(
        pack_body,
        out_shape=[jax.ShapeDtypeStruct((slots, rows // parts, channels), BF)] * parts,
        grid_spec=pltpu.PrefetchScalarGridSpec(
            num_scalar_prefetch=1,
            grid=(),
            in_specs=[pl.BlockSpec(memory_space=pltpu.VMEM)],
            out_specs=[pl.BlockSpec(memory_space=pltpu.VMEM)] * parts,
        ),
        compiler_params=pltpu.CompilerParams(vmem_limit_bytes=48 << 20),
        name="pack",
    )(slot, contrib)


def deposit_body(target_ref, *refs):
    pieces, o_ref = refs[:-1], refs[-1]
    o_ref[...] = jnp.zeros_like(o_ref)
    slots = pieces[0].shape[0]

    def step(s, _):
        t = target_ref[s]

        @pl.when(t >= 0)
        def _():
            at = 0
            for p in pieces:
                rows = pl.ds(at, p.shape[1])
                o_ref[t, rows, :] = o_ref[t, rows, :] + p[s].astype(F32)
                at += p.shape[1]

        return 0

    lax.fori_loop(0, slots, step, 0)


def deposit(target, pieces, blocks):
    rows = sum(p.shape[1] for p in pieces)
    channels = pieces[0].shape[2]
    return pl.pallas_call(
        deposit_body,
        out_shape=jax.ShapeDtypeStruct((blocks, rows, channels), F32),
        grid_spec=pltpu.PrefetchScalarGridSpec(
            num_scalar_prefetch=1,
            grid=(),
            in_specs=[pl.BlockSpec(memory_space=pltpu.VMEM)] * len(pieces),
            out_specs=pl.BlockSpec(memory_space=pltpu.VMEM),
        ),
        compiler_params=pltpu.CompilerParams(vmem_limit_bytes=48 << 20),
        name="deposit",
    )(target, *pieces)


def finish_body(core_ref, own_ref, got_ref, dep_ref, o_ref):
    half = own_ref.shape[2]
    mine = pl.ds(pl.multiple_of(core_ref[0] * half, half), half)
    other = pl.ds(pl.multiple_of((1 - core_ref[0]) * half, half), half)
    o_ref[:, :, mine] = own_ref[...].astype(F32) + dep_ref[:, :, mine]
    o_ref[:, :, other] = got_ref[...].astype(F32) + dep_ref[:, :, other]


def finish(core, own, got, dep):
    lat, lon, half = own.shape
    return pl.pallas_call(
        finish_body,
        out_shape=jax.ShapeDtypeStruct(dep.shape, F32),
        grid_spec=pltpu.PrefetchScalarGridSpec(
            num_scalar_prefetch=1,
            grid=(lat,),
            in_specs=[
                pl.BlockSpec((1, lon, half), lambda i, c: (i, 0, 0)),
                pl.BlockSpec((1, lon, half), lambda i, c: (i, 0, 0)),
                pl.BlockSpec((1, lon, 2 * half), lambda i, c: (i, 0, 0)),
            ],
            out_specs=pl.BlockSpec((1, lon, 2 * half), lambda i, c: (i, 0, 0)),
        ),
        name="finish",
    )(core, own, got, dep)


def shards(
    grid_adjoint_fields,
    interp_weights,
    depart_owner,
    depart_block,
    wave_perm,
    legendre,
    mode_proj,
    mode_back,
    mode_depth,
):
    x = grid_adjoint_fields
    wide = lax.axis_size("wide")
    narrow = lax.axis_size("narrow")
    w = lax.axis_index("wide")
    v = lax.axis_index("narrow")
    y, core = v // 2, v % 2
    ring = narrow // 2
    lat, lon, channels = x.shape
    half = channels // 2
    slots, lat_total, degrees = legendre.shape
    swap = [(i, i ^ 1) for i in range(narrow)]
    up = [(i, (i + 2) % narrow) for i in range(narrow)]
    down = [(i, (i - 2) % narrow) for i in range(narrow)]
    core_ids = core[None].astype(jnp.int32)

    x_other = jnp.where(core == 0, x[:, :, half:], x[:, :, :half])
    x_got = lax.ppermute(x_other, "narrow", swap)

    order = wave_perm.reshape(wide, ring, 2, slots).transpose(1, 2, 3, 0).reshape(ring, 2, 1, slots * wide)
    order = jnp.concatenate([order, order], axis=0)
    order = jnp.concatenate([order, order[:, :1]], axis=1)
    order = lax.dynamic_slice(order, (y, core, 0, 0), (ring, 2, 1, slots * wide))
    wave = jnp.broadcast_to(order, (ring, 2, 2, slots * wide)).reshape(-1).astype(F32)
    shift = jnp.broadcast_to(
        jnp.array([0.0, 640.0], F32)[None, None, :, None], (ring, 2, 2, slots * wide)
    ).reshape(-1)
    lons = jnp.arange(2 * lon, dtype=jnp.int32) % lon
    side = jnp.arange(2 * lon, dtype=jnp.int32) // lon
    lons = (lons + lon * jnp.where(side == 0, v, v ^ 1)).astype(F32)

    def table(columns):
        return cosine_of_phase(wave[columns][:, None] * lons[None, :] - shift[columns][:, None])

    def table_t(rows):
        return cosine_of_phase(wave[None, :] * lons[rows][:, None] - shift[None, :])

    per = 256
    far_a, far_b = dft(core_ids, table(slice(2 * per, 3 * per)), x, x_got, 4)
    near = jnp.concatenate([wave[3 * per :], wave[: 2 * per]])
    near = cosine_of_phase(
        near[:, None] * lons[None, :] - jnp.concatenate([shift[3 * per :], shift[: 2 * per]])[:, None]
    )
    down_a, down_b, own_a, own_b, up_a, up_b = dft(core_ids, near, x, x_got, 4)

    x_late, own_a = lax.optimization_barrier((x, own_a))
    blocks = interp_weights.shape[0]
    contrib = jnp.einsum(
        "bai,bac->bic", interp_weights, x_late.reshape(blocks, BS, channels), preferred_element_type=F32
    ).astype(BF)
    owner = depart_owner[:, 0]
    ids = jnp.arange(blocks, dtype=jnp.int32)
    rank = jnp.sum(
        ((owner[:, None] == owner[None, :]) & (ids[None, :] < ids[:, None])).astype(jnp.int32), axis=1
    )
    slot = owner * CAP + rank
    pick = jnp.arange(wide * CAP, dtype=jnp.int32)[:, None] == slot[None, :]
    target = jnp.max(jnp.where(pick, depart_block[None, :], -1), axis=1)
    packed = pack(slot, contrib, wide * CAP, 2)

    def send_deposit(piece):
        piece = piece.reshape(wide, CAP * piece.shape[1], channels)
        out = lax.all_to_all(piece, "wide", split_axis=0, concat_axis=0, tiled=True)
        return out.reshape(wide * CAP, -1, channels)

    got_1 = send_deposit(packed[0])

    relay_a = lax.ppermute(far_a, "narrow", up)
    relay_b = lax.ppermute(far_b, "narrow", down)
    direct_b = lax.ppermute(up_b, "narrow", up)
    direct_a = lax.ppermute(down_a, "narrow", down)
    sum_a = lax.ppermute((relay_a.astype(F32) + up_a.astype(F32)).astype(BF), "narrow", up)
    sum_b = lax.ppermute((relay_b.astype(F32) + down_b.astype(F32)).astype(BF), "narrow", down)
    marks = jnp.pad(
        target.reshape(wide, 1, CAP).astype(BF), ((0, 0), (0, lat - 1), (0, 128 - CAP))
    )
    rows = to_rows([own_a, sum_a, direct_a, own_b, sum_b, direct_b], marks, wide)
    rows, got_1 = lax.optimization_barrier((rows, got_1))
    rows = lax.all_to_all(rows, "wide", split_axis=0, concat_axis=0, tiled=True)
    other = lax.ppermute(rows[:, :, 2 * channels : 4 * channels], "narrow", swap)
    targets = rows[:, 0, 4 * channels : 4 * channels + CAP].astype(jnp.int32).reshape(wide * CAP)

    wavenumber = lax.dynamic_slice(wave_perm, ((w * narrow + v) * slots,), (slots,))
    degree_ids = jnp.arange(degrees, dtype=jnp.int32)
    masked = jnp.where(
        degree_ids[None, None, :] >= wavenumber[:, None, None], legendre, jnp.zeros_like(legendre)
    )
    masked_t = masked.transpose(0, 2, 1)
    degree = jnp.arange(degrees, dtype=F32)
    damp = 1.0 / (1.0 + (degree * (degree + 1.0))[:, None] * mode_depth[None, :])
    proj = jnp.where(core == 0, mode_proj, jnp.roll(mode_proj, half, axis=0)).astype(BF)
    back = jnp.where(core == 0, mode_back, jnp.roll(mode_back, half, axis=1)).astype(BF)
    synth = modes(
        rows.reshape(lat_total, -1), other.reshape(lat_total, -1), masked_t, masked, proj, back,
        damp, wide, lat,
    )
    synth = lax.all_to_all(synth, "wide", split_axis=0, concat_axis=0, tiled=True)
    second_piece, synth = lax.optimization_barrier((packed[1], synth))
    got_2 = send_deposit(second_piece)

    block_a, block_b = to_columns(synth, lax.ppermute(synth[:, 1], "narrow", swap))
    below_a = lax.ppermute(block_a, "narrow", up)
    above_b = lax.ppermute(block_b, "narrow", down)
    below_b = lax.ppermute(block_b, "narrow", up)
    above_a = lax.ppermute(block_a, "narrow", down)
    across_a = lax.ppermute(below_a, "narrow", up)
    across_b = lax.ppermute(above_b, "narrow", down)
    pieces = [block_a, block_b, above_a, above_b, across_a, across_b, below_a, below_b]
    wave_got = lax.ppermute(idft(table_t(slice(lon, 2 * lon)), pieces, 4), "narrow", swap)
    wave_own = idft(table_t(slice(0, lon)), pieces, 4)
    dep = deposit(targets, [got_1, got_2], blocks).reshape(lat, lon, channels)
    return finish(core_ids, wave_own, wave_got, dep)


def solution(mesh):
    in_specs = (
        P("wide", "narrow", None),
        P(("wide", "narrow"), None, None),
        P(("wide", "narrow"), None),
        P(("wide", "narrow")),
        P(),
        P(("wide", "narrow"), None, None),
        P(),
        P(),
        P(),
    )
    out_specs = P("wide", "narrow", None)
    return jax.shard_map(shards, mesh=mesh, in_specs=in_specs, out_specs=out_specs, check_vma=False)
```

```python
import math

import numpy as np
import jax
import jax.numpy as jnp
from jax import lax
from jax.experimental import pallas as pl
from jax.experimental.pallas import tpu as pltpu
from jax.sharding import PartitionSpec as P

NLON = 2560
BS = 32
CAP = 5
COUNTS = (2, 3)
BF = jnp.bfloat16
F32 = jnp.float32


def _half_sine_coefficients():
    nodes = (np.cos(np.pi * (np.arange(64) + 0.5) / 64) + 1) * 0.5 * (np.pi / 2) ** 2
    root = np.sqrt(nodes)
    return [float(c) for c in np.polynomial.polynomial.polyfit(nodes, np.sin(root) / root, 5)]


SINE = _half_sine_coefficients()


def cosine_of_phase(phase):
    turns = jnp.round(phase * (1.0 / NLON))
    u = (phase - turns * NLON) * (math.pi / NLON)
    z = u * u
    poly = jnp.full_like(z, SINE[-1])
    for coefficient in SINE[-2::-1]:
        poly = poly * z + coefficient
    s = u * poly
    return (1.0 - 2.0 * s * s).astype(BF)


def hbm(value):
    return pltpu.with_memory_space_constraint(value, pltpu.HBM)


def half_body(side_ref, x_ref, o_ref):
    o_ref[...] = x_ref[...]


def take_half(side, x):
    lat, lon, channels = x.shape
    half = channels // 2
    step = lat // 2
    return pl.pallas_call(
        half_body,
        out_shape=jax.ShapeDtypeStruct((lat, lon, half), BF),
        grid_spec=pltpu.PrefetchScalarGridSpec(
            num_scalar_prefetch=1,
            grid=(lat // step,),
            in_specs=[pl.BlockSpec((step, lon, half), lambda i, c: (i, 0, c[0]))],
            out_specs=pl.BlockSpec((step, lon, half), lambda i, c: (i, 0, 0)),
        ),
        name="take_half",
    )(side, x)


def dft_body(core_ref, t_ref, own_ref, got_ref, *outs):
    for lat in range(own_ref.shape[0]):
        x = jnp.concatenate([own_ref[lat], got_ref[lat]], axis=0)
        r = jnp.dot(t_ref[...], x, preferred_element_type=F32)
        for i, o in enumerate(outs):
            o[lat] = r[128 * i : 128 * i + 128].astype(BF)


def dft(core, table, x, got, step):
    rows = table.shape[0]
    lat, lon, channels = x.shape
    half = channels // 2
    n = rows // 128
    return pl.pallas_call(
        dft_body,
        out_shape=[jax.ShapeDtypeStruct((lat, 128, half), BF)] * n,
        grid_spec=pltpu.PrefetchScalarGridSpec(
            num_scalar_prefetch=1,
            grid=(lat // step,),
            in_specs=[
                pl.BlockSpec((rows, 2 * lon), lambda i, c: (0, 0)),
                pl.BlockSpec((step, lon, half), lambda i, c: (i, 0, c[0])),
                pl.BlockSpec((step, lon, half), lambda i, c: (i, 0, 0)),
            ],
            out_specs=[pl.BlockSpec((step, 128, half), lambda i, c: (i, 0, 0))] * n,
        ),
        compiler_params=pltpu.CompilerParams(vmem_limit_bytes=48 << 20),
        name="dft",
    )(core, table, x, got)


def rows_body(own_a, sum_a, direct_a, own_b, sum_b, direct_b, marks, o_hbm, o_other, o_mine, tmp, sem):
    wide, lat, width = o_mine.shape
    copies = [
        pltpu.make_async_copy(marks, o_hbm.at[:, :, pl.ds(2 * width, 128)], sem.at[0]),
        pltpu.make_async_copy(o_mine, o_hbm.at[:, :, pl.ds(0, width)], sem.at[1]),
    ]
    copies[0].start()
    half = own_a.shape[2]
    for s, parts in enumerate(((own_a, sum_a, direct_a), (own_b, sum_b, direct_b))):
        for q in range(4):
            for h in range(half // 128):
                t = tmp.at[(q * (half // 128) + h) % 4]
                lanes = slice(128 * h, 128 * h + 128)
                for l in range(lat):
                    value = sum(p[l, wide * q : wide * q + wide, lanes].astype(F32) for p in parts)
                    value = value * NLON ** (-0.5)
                    for j in range(wide // 8):
                        t[pl.ds(lat * 8 * j + l, 8, stride=lat), :] = value[8 * j : 8 * j + 8]
                col = q * half + 128 * h
                o_ref = (o_mine, o_other)[s]
                o_ref[:, :, col : col + 128] = t[...].astype(BF).reshape(wide, lat, 128)
        if s == 0:
            copies[1].start()
    for c in copies:
        c.wait()


def to_rows(pieces, marks, wide):
    lat, _, half = pieces[0].shape
    part = jax.ShapeDtypeStruct((wide, lat, 4 * half), BF)
    whole = jax.ShapeDtypeStruct((wide, lat, 8 * half + 128), BF)
    vmem, free = pl.BlockSpec(memory_space=pltpu.VMEM), pl.BlockSpec(memory_space=pl.ANY)
    return pl.pallas_call(
        rows_body,
        out_shape=[whole, part],
        in_specs=[vmem] * 7,
        out_specs=[free, vmem],
        scratch_shapes=[
            pltpu.VMEM(part.shape, BF),
            pltpu.VMEM((4, wide * lat, 128), F32),
            pltpu.SemaphoreType.DMA((2,)),
        ],
        compiler_params=pltpu.CompilerParams(vmem_limit_bytes=48 << 20),
        name="to_rows",
    )(*pieces, marks)


def join_body(rows_ref, got_ref, o_ref, sem):
    wide, _, width = got_ref.shape
    part = wide // 4
    copies = [
        pltpu.make_async_copy(
            got_ref.at[pl.ds(part * i, part)],
            o_ref.at[pl.ds(part * i, part), :, pl.ds(width, width)],
            sem.at[i],
        )
        for i in range(4)
    ]
    for c in copies:
        c.start()
    for c in copies:
        c.wait()


def join(rows, got):
    free = pl.BlockSpec(memory_space=pl.ANY)
    return pl.pallas_call(
        join_body,
        out_shape=jax.ShapeDtypeStruct(rows.shape, BF),
        in_specs=[free, pl.BlockSpec(memory_space=pltpu.VMEM)],
        out_specs=free,
        input_output_aliases={0: 0},
        scratch_shapes=[pltpu.SemaphoreType.DMA((4,))],
        name="join",
    )(rows, got)


def modes_body(ids_ref, fa_ref, fb_ref, fc_ref, fd_ref, leg_ref, p0_ref, p1_ref, b0_ref, b1_ref, depth_ref, o_ref, damp_ref):
    half = fa_ref.shape[1]
    degrees = leg_ref.shape[2]

    @pl.when(pl.program_id(0) == 0)
    def _():
        n = lax.broadcasted_iota(jnp.int32, damp_ref.shape, 0).astype(F32)
        damp_ref[...] = 1.0 / (1.0 + n * (n + 1.0) * depth_ref[...])

    degree = lax.broadcasted_iota(jnp.int32, leg_ref.shape[1:], 1)
    leg = leg_ref[0].astype(F32)
    leg = jnp.where(degree >= ids_ref[1 + pl.program_id(0)], leg, jnp.zeros_like(leg))
    turned = leg.T.astype(BF)
    leg = leg.astype(BF)
    spectra = [
        jnp.dot(turned, f[...], preferred_element_type=F32).astype(BF)
        for f in (fa_ref, fb_ref, fc_ref, fd_ref)
    ]
    low = jnp.concatenate([spectra[0], spectra[2]], axis=0)
    high = jnp.concatenate([spectra[1], spectra[3]], axis=0)
    modal = jnp.dot(low, p0_ref[...], preferred_element_type=F32)
    modal += jnp.dot(high, p1_ref[...], preferred_element_type=F32)
    modal = jnp.concatenate(
        [(modal[degrees * p : degrees * p + degrees] * damp_ref[...]).astype(BF) for p in range(2)], axis=0
    )
    wide, _, lat, _ = o_ref.shape
    for i, b_ref in enumerate((b0_ref, b1_ref)):
        back = jnp.dot(modal, b_ref[...], preferred_element_type=F32).astype(BF)
        for p in range(2):
            synth = jnp.dot(leg, back[degrees * p : degrees * p + degrees], preferred_element_type=F32)
            o_ref[:, i, :, half * p : half * p + half] = synth.astype(BF).reshape(wide, lat, half)


def modes(ids, f, legendre, proj, back, depth, wide, lat):
    slots, total, degrees = legendre.shape
    channels = proj.shape[0]
    half = channels // 2
    part = [pl.BlockSpec((total, half), lambda k, c, j=j: (0, j + 2 * k)) for j in (0, 4, 1, 5)]
    return pl.pallas_call(
        modes_body,
        out_shape=jax.ShapeDtypeStruct((wide, 2, lat, 4 * half), BF),
        grid_spec=pltpu.PrefetchScalarGridSpec(
            num_scalar_prefetch=1,
            grid=(slots,),
            in_specs=part
            + [
                pl.BlockSpec((1, total, degrees), lambda k, c: (k, 0, 0)),
                pl.BlockSpec((half, channels), lambda k, c: (c[0], 0)),
                pl.BlockSpec((half, channels), lambda k, c: (1 - c[0], 0)),
                pl.BlockSpec((channels, half), lambda k, c: (0, c[0])),
                pl.BlockSpec((channels, half), lambda k, c: (0, 1 - c[0])),
                pl.BlockSpec((1, channels), lambda k, c: (0, 0)),
            ],
            out_specs=pl.BlockSpec((wide, 2, lat, 2 * half), lambda k, c: (0, 0, 0, k)),
            scratch_shapes=[pltpu.VMEM((degrees, channels), F32)],
        ),
        compiler_params=pltpu.CompilerParams(vmem_limit_bytes=48 << 20),
        name="modes",
    )(ids, f, f, f, f, legendre, proj, proj, back, back, depth)


def columns_body(keep, take, o_ref, tmp):
    wide, lat, _ = take.shape
    half = o_ref.shape[3]
    for s, src in enumerate((keep, take)):
        for q in range(4):
            for h in range(half // 128):
                t = tmp.at[(q * (half // 128) + h) % 4]
                col = slice(half * q + 128 * h, half * q + 128 * h + 128)
                value = src[:, 0, :, col] if s == 0 else src[:, :, col]
                t[...] = value.astype(F32).reshape(wide * lat, 128)
                for l in range(lat):
                    rows = [t[pl.ds(lat * 8 * j + l, 8, stride=lat), :] for j in range(wide // 8)]
                    rows = jnp.concatenate(rows, axis=0).astype(BF)
                    o_ref[s, l, wide * q : wide * q + wide, 128 * h : 128 * h + 128] = rows


def to_columns(keep, take):
    wide, lat, width = take.shape
    half = width // 4
    return pl.pallas_call(
        columns_body,
        out_shape=jax.ShapeDtypeStruct((2, lat, 4 * wide, half), BF),
        grid=(1,),
        in_specs=[
            pl.BlockSpec((wide, 1, lat, width), lambda i: (0, 0, 0, 0)),
            pl.BlockSpec((wide, lat, width), lambda i: (0, 0, 0)),
        ],
        out_specs=pl.BlockSpec((2, lat, 4 * wide, half), lambda i: (0, 0, 0, 0)),
        scratch_shapes=[pltpu.VMEM((4, wide * lat, 128), F32)],
        compiler_params=pltpu.CompilerParams(vmem_limit_bytes=48 << 20),
        name="to_columns",
    )(keep, take)


def idft_body(t_ref, own, above, across_a, across_b, below, o_ref):
    for lat in range(o_ref.shape[0]):
        g = [own[0, lat], own[1, lat], above[0, lat], above[1, lat]]
        g += [across_a[lat], across_b[lat], below[0, lat], below[1, lat]]
        r = jnp.dot(t_ref[...], jnp.concatenate(g, axis=0), preferred_element_type=F32)
        o_ref[lat] = (r * NLON ** (-0.5)).astype(BF)


def idft(table, own, above, across_a, across_b, below, step):
    _, lat, rows, half = own.shape
    lon = table.shape[0]
    pair = pl.BlockSpec((2, step, rows, half), lambda i: (0, i, 0, 0))
    single = pl.BlockSpec((step, rows, half), lambda i: (i, 0, 0))
    return pl.pallas_call(
        idft_body,
        out_shape=jax.ShapeDtypeStruct((lat, lon, half), BF),
        grid=(lat // step,),
        in_specs=[pl.BlockSpec(table.shape, lambda i: (0, 0)), pair, pair, single, single, pair],
        out_specs=pl.BlockSpec((step, lon, half), lambda i: (i, 0, 0)),
        compiler_params=pltpu.CompilerParams(vmem_limit_bytes=48 << 20),
        name="idft",
    )(table, own, above, across_a, across_b, below)


def pack(owner, rank, contrib, owners, first, count):
    blocks, rows, channels = contrib.shape

    def body(owner_ref, rank_ref, contrib_ref, o_ref):
        def step(b, _):
            r = rank_ref[b] - first

            @pl.when((r >= 0) & (r < count))
            def _():
                o_ref[owner_ref[b], r] = contrib_ref[b]

            return 0

        lax.fori_loop(0, blocks, step, 0)

    return pl.pallas_call(
        body,
        out_shape=jax.ShapeDtypeStruct((owners, count, rows, channels), BF),
        grid_spec=pltpu.PrefetchScalarGridSpec(
            num_scalar_prefetch=2,
            grid=(),
            in_specs=[pl.BlockSpec(memory_space=pltpu.VMEM)],
            out_specs=pl.BlockSpec(memory_space=pltpu.VMEM),
        ),
        compiler_params=pltpu.CompilerParams(vmem_limit_bytes=48 << 20),
        name="pack",
    )(owner, rank, contrib)


def finish(core, own, got, lists, pieces):
    lat, lon, half = own.shape
    n = len(pieces)
    blocks = lon // BS

    def body(core_ref, start, order, target, own_hbm, got_hbm, *refs):
        pieces_hbm, (o_hbm, own_ref, got_ref, out, sem, out_sem) = refs[:n], refs[n : n + 6]
        piece_refs = refs[n + 6 :]
        copies, k = [], 0
        for p, dst in zip(pieces_hbm, piece_refs):
            part = p.shape[0] // 4
            for j in range(4):
                rows = pl.ds(j * part, part)
                copies.append(pltpu.make_async_copy(p.at[rows], dst.at[rows], sem.at[k]))
                k += 1
        for src, dst in ((own_hbm, own_ref), (got_hbm, got_ref)):
            for j in range(2):
                rows = pl.ds(j * (lat // 2), lat // 2)
                copies.append(pltpu.make_async_copy(src.at[rows], dst.at[rows], sem.at[k]))
                k += 1
        for c in copies:
            c.start()
        for c in copies:
            c.wait()
        mine = pl.ds(pl.multiple_of(core_ref[0] * half, half), half)
        other = pl.ds(pl.multiple_of((1 - core_ref[0]) * half, half), half)

        def write(i):
            return pltpu.make_async_copy(out.at[i], o_hbm.at[i], out_sem.at[i])

        def latitude(i, _):
            out[i, :, mine] = own_ref[i].astype(F32)
            out[i, :, other] = got_ref[i].astype(F32)

            for p, piece in enumerate(piece_refs):

                def step(e, _):
                    s = order[p, e]
                    rows = pl.ds(pl.multiple_of((target[p, s] - i * blocks) * BS, BS), BS)
                    out[i, rows, :] = out[i, rows, :] + piece[s].astype(F32)
                    return 0

                lax.fori_loop(start[p, i], start[p, i + 1], step, 0)
            write(i).start()
            return 0

        lax.fori_loop(0, lat, latitude, 0)
        for i in range(lat):
            write(i).wait()

    return pl.pallas_call(
        body,
        out_shape=jax.ShapeDtypeStruct((lat, lon, 2 * half), F32),
        grid_spec=pltpu.PrefetchScalarGridSpec(
            num_scalar_prefetch=4,
            grid=(),
            in_specs=[pl.BlockSpec(memory_space=pl.ANY)] * (2 + n),
            out_specs=pl.BlockSpec(memory_space=pl.ANY),
            scratch_shapes=[
                pltpu.VMEM((lat, lon, half), BF),
                pltpu.VMEM((lat, lon, half), BF),
                pltpu.VMEM((lat, lon, 2 * half), F32),
                pltpu.SemaphoreType.DMA((4 + 4 * n,)),
                pltpu.SemaphoreType.DMA((lat,)),
            ]
            + [pltpu.VMEM(p.shape, BF) for p in pieces],
        ),
        compiler_params=pltpu.CompilerParams(vmem_limit_bytes=48 << 20),
        name="finish",
    )(core, *lists, own, got, *pieces)


def by_latitude(target, lat, blocks):
    ids = jnp.arange(target.shape[0], dtype=jnp.int32)
    before = (target[None, :] < target[:, None]) | (
        (target[None, :] == target[:, None]) & (ids[None, :] < ids[:, None])
    )
    place = jnp.sum(before.astype(jnp.int32), axis=1)
    order = jnp.sum(jnp.where(place[None, :] == ids[:, None], ids[None, :], 0), axis=1)
    first = jnp.arange(lat + 1, dtype=jnp.int32) * blocks
    start = jnp.sum((target[None, :] < first[:, None]).astype(jnp.int32), axis=1)
    return start, order, target


def shards(
    grid_adjoint_fields,
    interp_weights,
    depart_owner,
    depart_block,
    wave_perm,
    legendre,
    mode_proj,
    mode_back,
    mode_depth,
):
    x = grid_adjoint_fields
    wide = lax.axis_size("wide")
    narrow = lax.axis_size("narrow")
    w = lax.axis_index("wide")
    v = lax.axis_index("narrow")
    y, core = v // 2, v % 2
    ring = narrow // 2
    lat, lon, channels = x.shape
    half = channels // 2
    slots, lat_total, degrees = legendre.shape
    swap = [(i, i ^ 1) for i in range(narrow)]
    up = [(i, (i + 2) % narrow) for i in range(narrow)]
    down = [(i, (i - 2) % narrow) for i in range(narrow)]
    core_ids = core[None].astype(jnp.int32)

    x_got = lax.ppermute(take_half(1 - core_ids, hbm(x)), "narrow", swap)

    order = wave_perm.reshape(wide, ring, 2, slots).transpose(1, 2, 3, 0)
    order = jnp.concatenate([order, order], axis=0)
    order = jnp.concatenate([order, order[:, :1]], axis=1)
    order = lax.dynamic_slice(order, (y, core, 0, 0), (ring, 2, slots, wide))[:, :, :, None]
    columns = (ring, 2, slots, 2, wide)
    wave = jnp.broadcast_to(order, columns).reshape(-1).astype(F32)
    shift = jnp.tile(jnp.repeat(jnp.array([0.0, 640.0], F32), wide), ring * 2 * slots)
    lons = jnp.arange(2 * lon, dtype=jnp.int32) % lon
    side = jnp.arange(2 * lon, dtype=jnp.int32) // lon
    lons = (lons + lon * jnp.where(side == 0, v, v ^ 1)).astype(F32)

    def table(columns):
        return cosine_of_phase(wave[columns][:, None] * lons[None, :] - shift[columns][:, None])

    def table_t(rows):
        return cosine_of_phase(wave[None, :] * lons[rows][:, None] - shift[None, :])

    blocks = interp_weights.shape[0]
    contrib = jnp.einsum(
        "bai,bac->bic", interp_weights, x.reshape(blocks, BS, channels), preferred_element_type=F32
    ).astype(BF)
    owner = depart_owner[:, 0]
    ids = jnp.arange(blocks, dtype=jnp.int32)
    rank = jnp.sum(
        ((owner[:, None] == owner[None, :]) & (ids[None, :] < ids[:, None])).astype(jnp.int32), axis=1
    )
    slot = owner * CAP + rank
    pick = jnp.arange(wide * CAP, dtype=jnp.int32)[:, None] == slot[None, :]
    target = jnp.max(jnp.where(pick, depart_block[None, :], -1), axis=1)
    cut = [0]
    for n in COUNTS:
        cut.append(cut[-1] + n)

    def send_deposit(piece):
        out = lax.all_to_all(
            piece.reshape(wide, -1, channels), "wide", split_axis=0, concat_axis=0, tiled=True
        )
        return out.reshape(-1, BS, channels)

    piece_1 = pack(owner, rank, contrib, wide, cut[0], COUNTS[0])
    got_1 = send_deposit(piece_1)

    per = 256
    x_late, piece_1 = lax.optimization_barrier((x, piece_1))
    x = x_late
    far_a, far_b = dft(core_ids, table(slice(2 * per, 3 * per)), x, x_got, 4)

    near = jnp.concatenate([wave[3 * per :], wave[: 2 * per]])
    near_shift = jnp.concatenate([shift[3 * per :], shift[: 2 * per]])
    near = cosine_of_phase(near[:, None] * lons[None, :] - near_shift[:, None])
    down_a, down_b, own_a, own_b, up_a, up_b = dft(core_ids, near, x, x_got, 4)

    relay_a = lax.ppermute(far_a, "narrow", up)
    relay_b = lax.ppermute(far_b, "narrow", down)
    direct_b = lax.ppermute(up_b, "narrow", up)
    direct_a = lax.ppermute(down_a, "narrow", down)
    sum_a = lax.ppermute((relay_a.astype(F32) + up_a.astype(F32)).astype(BF), "narrow", up)
    sum_b = lax.ppermute((relay_b.astype(F32) + down_b.astype(F32)).astype(BF), "narrow", down)
    marks = jnp.pad(
        target.reshape(wide, 1, CAP).astype(BF), ((0, 0), (0, lat - 1), (0, 128 - CAP))
    )
    slot_waves = lax.dynamic_slice(wave_perm, ((w * narrow + v) * slots,), (slots,))
    mode_ids = jnp.concatenate([core_ids, slot_waves])
    proj, back = mode_proj.astype(BF), mode_back.astype(BF)
    piece_2 = pack(owner, rank, contrib, wide, cut[1], COUNTS[1])
    own_a, piece_2, proj, back, marks = lax.optimization_barrier(
        (own_a, piece_2, proj, back, marks)
    )
    rows, other = to_rows([own_a, sum_a, direct_a, own_b, sum_b, direct_b], marks, wide)
    rows = join(rows, lax.ppermute(other, "narrow", swap))
    rows, got_1 = lax.optimization_barrier((rows, got_1))
    rows = lax.all_to_all(rows, "wide", split_axis=0, concat_axis=0, tiled=True)
    targets = rows[:, 0, 4 * channels : 4 * channels + CAP].astype(jnp.int32)
    most = wide * max(COUNTS)
    lists = []
    for a, b in zip(cut, cut[1:]):
        part = targets[:, a:b].reshape(-1)
        lists.append(by_latitude(jnp.pad(part, (0, most - part.shape[0]), constant_values=-1), lat, lon // BS))
    lists = [jnp.stack(group) for group in zip(*lists)]
    synth = modes(
        mode_ids, rows.reshape(lat_total, -1), hbm(legendre), hbm(proj), hbm(back),
        mode_depth.reshape(1, -1), wide, lat,
    )
    synth = lax.all_to_all(synth, "wide", split_axis=0, concat_axis=0, tiled=True)
    piece_2, synth = lax.optimization_barrier((piece_2, synth))
    got_2 = send_deposit(piece_2)

    own = to_columns(synth, lax.ppermute(synth[:, 1], "narrow", swap))
    below = lax.ppermute(own, "narrow", up)
    above = lax.ppermute(own, "narrow", down)
    across_a = lax.ppermute(below[0], "narrow", up)
    across_b = lax.ppermute(above[1], "narrow", down)
    pieces = [own, above, across_a, across_b, below]
    wave_got = lax.ppermute(idft(table_t(slice(lon, 2 * lon)), *pieces, 4), "narrow", swap)
    wave_own = idft(table_t(slice(0, lon)), *pieces, 4)
    return finish(core_ids, wave_own, wave_got, lists, [hbm(got_1), hbm(got_2)])


def solution(mesh):
    in_specs = (
        P("wide", "narrow", None),
        P(("wide", "narrow"), None, None),
        P(("wide", "narrow"), None),
        P(("wide", "narrow")),
        P(),
        P(("wide", "narrow"), None, None),
        P(),
        P(),
        P(),
    )
    out_specs = P("wide", "narrow", None)
    return jax.shard_map(shards, mesh=mesh, in_specs=in_specs, out_specs=out_specs, check_vma=False)
```

```python
import math

import numpy as np
import jax
import jax.numpy as jnp
from jax import lax
from jax.experimental import pallas as pl
from jax.experimental.pallas import tpu as pltpu
from jax.sharding import PartitionSpec as P

NLON = 2560
BS = 32
CAP = 5
COUNTS = (2, 3)
BF = jnp.bfloat16
F32 = jnp.float32


def _half_sine_coefficients():
    nodes = (np.cos(np.pi * (np.arange(64) + 0.5) / 64) + 1) * 0.5 * (np.pi / 2) ** 2
    root = np.sqrt(nodes)
    return [float(c) for c in np.polynomial.polynomial.polyfit(nodes, np.sin(root) / root, 5)]


SINE = _half_sine_coefficients()


def cosine_of_phase(phase):
    turns = jnp.round(phase * (1.0 / NLON))
    u = (phase - turns * NLON) * (math.pi / NLON)
    z = u * u
    poly = jnp.full_like(z, SINE[-1])
    for coefficient in SINE[-2::-1]:
        poly = poly * z + coefficient
    s = u * poly
    return (1.0 - 2.0 * s * s).astype(BF)


def hbm(value):
    return pltpu.with_memory_space_constraint(value, pltpu.HBM)


def vmem(value):
    return pltpu.with_memory_space_constraint(value, pltpu.VMEM)


def half_body(side_ref, x_ref, o_ref):
    o_ref[...] = x_ref[...]


def take_half(side, x):
    lat, lon, channels = x.shape
    half = channels // 2
    step = lat // 2
    return pl.pallas_call(
        half_body,
        out_shape=jax.ShapeDtypeStruct((lat, lon, half), BF),
        grid_spec=pltpu.PrefetchScalarGridSpec(
            num_scalar_prefetch=1,
            grid=(lat // step,),
            in_specs=[pl.BlockSpec((step, lon, half), lambda i, c: (i, 0, c[0]))],
            out_specs=pl.BlockSpec((step, lon, half), lambda i, c: (i, 0, 0)),
        ),
        name="take_half",
    )(side, x)


def dft_body(core_ref, t_ref, own_ref, got_ref, *outs):
    for lat in range(own_ref.shape[0]):
        x = jnp.concatenate([own_ref[lat], got_ref[lat]], axis=0)
        r = jnp.dot(t_ref[...], x, preferred_element_type=F32)
        for i, o in enumerate(outs):
            o[lat] = r[128 * i : 128 * i + 128].astype(BF)


def dft(core, table, x, got, step):
    rows = table.shape[0]
    lat, lon, channels = x.shape
    half = channels // 2
    n = rows // 128
    return pl.pallas_call(
        dft_body,
        out_shape=[jax.ShapeDtypeStruct((lat, 128, half), BF)] * n,
        grid_spec=pltpu.PrefetchScalarGridSpec(
            num_scalar_prefetch=1,
            grid=(lat // step,),
            in_specs=[
                pl.BlockSpec((rows, 2 * lon), lambda i, c: (0, 0)),
                pl.BlockSpec((step, lon, half), lambda i, c: (i, 0, c[0])),
                pl.BlockSpec((step, lon, half), lambda i, c: (i, 0, 0)),
            ],
            out_specs=[pl.BlockSpec((step, 128, half), lambda i, c: (i, 0, 0))] * n,
        ),
        compiler_params=pltpu.CompilerParams(vmem_limit_bytes=48 << 20),
        name="dft",
    )(core, table, x, got)


def rows_body(own_a, sum_a, direct_a, own_b, sum_b, direct_b, marks, o_hbm, o_other, o_mine, tmp, sem):
    wide, lat, width = o_mine.shape
    copies = [
        pltpu.make_async_copy(marks, o_hbm.at[:, :, pl.ds(2 * width, 128)], sem.at[0]),
        pltpu.make_async_copy(o_mine, o_hbm.at[:, :, pl.ds(0, width)], sem.at[1]),
    ]
    copies[0].start()
    half = own_a.shape[2]
    for s, parts in enumerate(((own_a, sum_a, direct_a), (own_b, sum_b, direct_b))):
        for q in range(4):
            for h in range(half // 128):
                t = tmp.at[(q * (half // 128) + h) % 4]
                lanes = slice(128 * h, 128 * h + 128)
                for l in range(lat):
                    value = sum(p[l, wide * q : wide * q + wide, lanes].astype(F32) for p in parts)
                    value = value * NLON ** (-0.5)
                    for j in range(wide // 8):
                        t[pl.ds(lat * 8 * j + l, 8, stride=lat), :] = value[8 * j : 8 * j + 8]
                col = q * half + 128 * h
                o_ref = (o_mine, o_other)[s]
                o_ref[:, :, col : col + 128] = t[...].astype(BF).reshape(wide, lat, 128)
        if s == 0:
            copies[1].start()
    for c in copies:
        c.wait()


def to_rows(pieces, marks, wide):
    lat, _, half = pieces[0].shape
    part = jax.ShapeDtypeStruct((wide, lat, 4 * half), BF)
    whole = pltpu.HBM((wide, lat, 8 * half + 128), BF)
    near, free = pl.BlockSpec(memory_space=pltpu.VMEM), pl.BlockSpec(memory_space=pl.ANY)
    return pl.pallas_call(
        rows_body,
        out_shape=[whole, part],
        in_specs=[near] * 7,
        out_specs=[free, near],
        scratch_shapes=[
            pltpu.VMEM(part.shape, BF),
            pltpu.VMEM((4, wide * lat, 128), F32),
            pltpu.SemaphoreType.DMA((2,)),
        ],
        compiler_params=pltpu.CompilerParams(vmem_limit_bytes=48 << 20),
        name="to_rows",
    )(*pieces, marks)


def join_body(rows_ref, got_ref, o_ref, sem):
    wide, _, width = got_ref.shape
    part = wide // 4
    copies = [
        pltpu.make_async_copy(
            got_ref.at[pl.ds(part * i, part)],
            o_ref.at[pl.ds(part * i, part), :, pl.ds(width, width)],
            sem.at[i],
        )
        for i in range(4)
    ]
    for c in copies:
        c.start()
    for c in copies:
        c.wait()


def join(rows, got):
    free = pl.BlockSpec(memory_space=pl.ANY)
    return pl.pallas_call(
        join_body,
        out_shape=pltpu.HBM(rows.shape, BF),
        in_specs=[free, pl.BlockSpec(memory_space=pltpu.VMEM)],
        out_specs=free,
        input_output_aliases={0: 0},
        scratch_shapes=[pltpu.SemaphoreType.DMA((4,))],
        name="join",
    )(rows, got)


def modes_body(ids_ref, fa_ref, fb_ref, fc_ref, fd_ref, leg_ref, p0_ref, p1_ref, b0_ref, b1_ref, depth_ref, o_ref, damp_ref):
    half = fa_ref.shape[1]
    degrees = leg_ref.shape[2]

    @pl.when(pl.program_id(0) == 0)
    def _():
        n = lax.broadcasted_iota(jnp.int32, damp_ref.shape, 0).astype(F32)
        damp_ref[...] = 1.0 / (1.0 + n * (n + 1.0) * depth_ref[...])

    degree = lax.broadcasted_iota(jnp.int32, leg_ref.shape[1:], 1)
    leg = leg_ref[0].astype(F32)
    leg = jnp.where(degree >= ids_ref[1 + pl.program_id(0)], leg, jnp.zeros_like(leg))
    turned = leg.T.astype(BF)
    leg = leg.astype(BF)
    spectra = [
        jnp.dot(turned, f[...], preferred_element_type=F32).astype(BF)
        for f in (fa_ref, fb_ref, fc_ref, fd_ref)
    ]
    low = jnp.concatenate([spectra[0], spectra[2]], axis=0)
    high = jnp.concatenate([spectra[1], spectra[3]], axis=0)
    modal = jnp.dot(low, p0_ref[...], preferred_element_type=F32)
    modal += jnp.dot(high, p1_ref[...], preferred_element_type=F32)
    modal = jnp.concatenate(
        [(modal[degrees * p : degrees * p + degrees] * damp_ref[...]).astype(BF) for p in range(2)], axis=0
    )
    wide, _, lat, _ = o_ref.shape
    for i, b_ref in enumerate((b0_ref, b1_ref)):
        back = jnp.dot(modal, b_ref[...], preferred_element_type=F32).astype(BF)
        for p in range(2):
            synth = jnp.dot(leg, back[degrees * p : degrees * p + degrees], preferred_element_type=F32)
            o_ref[:, i, :, half * p : half * p + half] = synth.astype(BF).reshape(wide, lat, half)


def modes(ids, f, legendre, proj, back, depth, wide, lat):
    slots, total, degrees = legendre.shape
    channels = proj.shape[0]
    half = channels // 2
    part = [pl.BlockSpec((total, half), lambda k, c, j=j: (0, j + 2 * k)) for j in (0, 4, 1, 5)]
    return pl.pallas_call(
        modes_body,
        out_shape=jax.ShapeDtypeStruct((wide, 2, lat, 4 * half), BF),
        grid_spec=pltpu.PrefetchScalarGridSpec(
            num_scalar_prefetch=1,
            grid=(slots,),
            in_specs=part
            + [
                pl.BlockSpec((1, total, degrees), lambda k, c: (k, 0, 0)),
                pl.BlockSpec((half, channels), lambda k, c: (c[0], 0)),
                pl.BlockSpec((half, channels), lambda k, c: (1 - c[0], 0)),
                pl.BlockSpec((channels, half), lambda k, c: (0, c[0])),
                pl.BlockSpec((channels, half), lambda k, c: (0, 1 - c[0])),
                pl.BlockSpec((1, channels), lambda k, c: (0, 0)),
            ],
            out_specs=pl.BlockSpec((wide, 2, lat, 2 * half), lambda k, c: (0, 0, 0, k)),
            scratch_shapes=[pltpu.VMEM((degrees, channels), F32)],
        ),
        compiler_params=pltpu.CompilerParams(vmem_limit_bytes=48 << 20),
        name="modes",
    )(ids, f, f, f, f, legendre, proj, proj, back, back, depth)


def columns_body(keep, take, o_ref, tmp):
    wide, lat, _ = take.shape
    half = o_ref.shape[3]
    for s, src in enumerate((keep, take)):
        for q in range(4):
            for h in range(half // 128):
                t = tmp.at[(q * (half // 128) + h) % 4]
                col = slice(half * q + 128 * h, half * q + 128 * h + 128)
                value = src[:, 0, :, col] if s == 0 else src[:, :, col]
                t[...] = value.astype(F32).reshape(wide * lat, 128)
                for l in range(lat):
                    rows = [t[pl.ds(lat * 8 * j + l, 8, stride=lat), :] for j in range(wide // 8)]
                    rows = jnp.concatenate(rows, axis=0).astype(BF)
                    o_ref[s, l, wide * q : wide * q + wide, 128 * h : 128 * h + 128] = rows


def to_columns(keep, take):
    wide, lat, width = take.shape
    half = width // 4
    return pl.pallas_call(
        columns_body,
        out_shape=jax.ShapeDtypeStruct((2, lat, 4 * wide, half), BF),
        grid=(1,),
        in_specs=[
            pl.BlockSpec((wide, 1, lat, width), lambda i: (0, 0, 0, 0)),
            pl.BlockSpec((wide, lat, width), lambda i: (0, 0, 0)),
        ],
        out_specs=pl.BlockSpec((2, lat, 4 * wide, half), lambda i: (0, 0, 0, 0)),
        scratch_shapes=[pltpu.VMEM((4, wide * lat, 128), F32)],
        compiler_params=pltpu.CompilerParams(vmem_limit_bytes=48 << 20),
        name="to_columns",
    )(keep, take)


def idft_body(t_ref, own, above, across_a, across_b, below, o_ref):
    for lat in range(o_ref.shape[0]):
        g = [own[0, lat], own[1, lat], above[0, lat], above[1, lat]]
        g += [across_a[lat], across_b[lat], below[0, lat], below[1, lat]]
        r = jnp.dot(t_ref[...], jnp.concatenate(g, axis=0), preferred_element_type=F32)
        o_ref[lat] = (r * NLON ** (-0.5)).astype(BF)


def idft(table, own, above, across_a, across_b, below, step):
    _, lat, rows, half = own.shape
    lon = table.shape[0]
    pair = pl.BlockSpec((2, step, rows, half), lambda i: (0, i, 0, 0))
    single = pl.BlockSpec((step, rows, half), lambda i: (i, 0, 0))
    return pl.pallas_call(
        idft_body,
        out_shape=jax.ShapeDtypeStruct((lat, lon, half), BF),
        grid=(lat // step,),
        in_specs=[pl.BlockSpec(table.shape, lambda i: (0, 0)), pair, pair, single, single, pair],
        out_specs=pl.BlockSpec((step, lon, half), lambda i: (i, 0, 0)),
        compiler_params=pltpu.CompilerParams(vmem_limit_bytes=48 << 20),
        name="idft",
    )(table, own, above, across_a, across_b, below)


def pack(owner, rank, contrib, owners, first, count):
    blocks, rows, channels = contrib.shape
    out_parts = 8
    out_size = owners // out_parts

    def body(owner_ref, rank_ref, contrib_ref, o_hbm, o_ref, out_sem):
        def step(b, _):
            r = rank_ref[b] - first

            @pl.when((r >= 0) & (r < count))
            def _():
                o_ref[owner_ref[b], r] = contrib_ref[b]

            return 0

        lax.fori_loop(0, blocks, step, 0)
        stores = []
        for i in range(out_parts):
            at = pl.ds(i * out_size, out_size)
            stores.append(pltpu.make_async_copy(o_ref.at[at], o_hbm.at[at], out_sem.at[i]))
            stores[-1].start()
        for c in stores:
            c.wait()

    out = (owners, count, rows, channels)
    return pl.pallas_call(
        body,
        out_shape=pltpu.HBM(out, BF),
        grid_spec=pltpu.PrefetchScalarGridSpec(
            num_scalar_prefetch=2,
            grid=(),
            in_specs=[pl.BlockSpec(memory_space=pltpu.VMEM)],
            out_specs=pl.BlockSpec(memory_space=pl.ANY),
            scratch_shapes=[
                pltpu.VMEM(out, BF),
                pltpu.SemaphoreType.DMA((out_parts,)),
            ],
        ),
        compiler_params=pltpu.CompilerParams(vmem_limit_bytes=48 << 20),
        name="pack",
    )(owner, rank, vmem(contrib))


def add_blocks(i, start, order, target, piece, out, blocks):
    def step(e, _):
        s = order[e]
        rows = pl.ds(pl.multiple_of((target[s] - i * blocks) * BS, BS), BS)
        out[i, rows, :] = out[i, rows, :] + piece[s].astype(F32)
        return 0

    lax.fori_loop(start[i], start[i + 1], step, 0)


def base(core, own, got, lists, piece):
    lat, lon, half = own.shape

    def body(core_ref, start, order, target, own_ref, got_ref, piece_ref, o_ref):
        mine = pl.ds(pl.multiple_of(core_ref[0] * half, half), half)
        other = pl.ds(pl.multiple_of((1 - core_ref[0]) * half, half), half)

        def latitude(i, _):
            o_ref[i, :, mine] = own_ref[i].astype(F32)
            o_ref[i, :, other] = got_ref[i].astype(F32)
            add_blocks(i, start, order, target, piece_ref, o_ref, lon // BS)
            return 0

        lax.fori_loop(0, lat, latitude, 0)

    return pl.pallas_call(
        body,
        out_shape=pltpu.HBM((lat, lon, 2 * half), F32),
        grid_spec=pltpu.PrefetchScalarGridSpec(
            num_scalar_prefetch=4,
            grid=(),
            in_specs=[pl.BlockSpec(memory_space=pltpu.VMEM)] * 3,
            out_specs=pl.BlockSpec(memory_space=pltpu.VMEM),
        ),
        compiler_params=pltpu.CompilerParams(vmem_limit_bytes=48 << 20),
        name="base",
    )(core, *lists, own, got, piece)


def finish(begun, lists, piece):
    lat, lon, channels = begun.shape

    slots = piece.shape[0]
    parts = 6
    size = slots // parts

    def body(start, order, target, begun_hbm, piece_hbm, o_hbm, out, piece_ref, sem, read_sem, piece_sem):
        loads = []
        for j in range(parts):
            at = pl.ds(j * size, size)
            loads.append(pltpu.make_async_copy(piece_hbm.at[at], piece_ref.at[at], piece_sem.at[j]))
            loads[-1].start()

        def read(i):
            return pltpu.make_async_copy(begun_hbm.at[i], out.at[i], read_sem.at[i])

        for i in range(lat):
            read(i).start()
        for c in loads:
            c.wait()

        def write(i):
            return pltpu.make_async_copy(out.at[i], o_hbm.at[i], sem.at[i])

        def latitude(i, _):
            read(i).wait()
            add_blocks(i, start, order, target, piece_ref, out, lon // BS)
            write(i).start()
            return 0

        lax.fori_loop(0, lat, latitude, 0)
        for i in range(lat):
            write(i).wait()

    return pl.pallas_call(
        body,
        out_shape=jax.ShapeDtypeStruct(begun.shape, F32),
        grid_spec=pltpu.PrefetchScalarGridSpec(
            num_scalar_prefetch=3,
            grid=(),
            in_specs=[pl.BlockSpec(memory_space=pl.ANY)] * 2,
            out_specs=pl.BlockSpec(memory_space=pl.ANY),
            scratch_shapes=[
                pltpu.VMEM(begun.shape, F32),
                pltpu.VMEM(piece.shape, BF),
                pltpu.SemaphoreType.DMA((lat,)),
                pltpu.SemaphoreType.DMA((lat,)),
                pltpu.SemaphoreType.DMA((parts,)),
            ],
        ),
        compiler_params=pltpu.CompilerParams(vmem_limit_bytes=48 << 20),
        name="finish",
    )(*lists, begun, piece)


def by_latitude(target, lat, blocks):
    ids = jnp.arange(target.shape[0], dtype=jnp.int32)
    before = (target[None, :] < target[:, None]) | (
        (target[None, :] == target[:, None]) & (ids[None, :] < ids[:, None])
    )
    place = jnp.sum(before.astype(jnp.int32), axis=1)
    order = jnp.sum(jnp.where(place[None, :] == ids[:, None], ids[None, :], 0), axis=1)
    first = jnp.arange(lat + 1, dtype=jnp.int32) * blocks
    start = jnp.sum((target[None, :] < first[:, None]).astype(jnp.int32), axis=1)
    return start, order, target


def shards(
    grid_adjoint_fields,
    interp_weights,
    depart_owner,
    depart_block,
    wave_perm,
    legendre,
    mode_proj,
    mode_back,
    mode_depth,
):
    x = grid_adjoint_fields
    wide = lax.axis_size("wide")
    narrow = lax.axis_size("narrow")
    w = lax.axis_index("wide")
    v = lax.axis_index("narrow")
    y, core = v // 2, v % 2
    ring = narrow // 2
    lat, lon, channels = x.shape
    half = channels // 2
    slots, lat_total, degrees = legendre.shape
    swap = [(i, i ^ 1) for i in range(narrow)]
    up = [(i, (i + 2) % narrow) for i in range(narrow)]
    down = [(i, (i - 2) % narrow) for i in range(narrow)]
    core_ids = core[None].astype(jnp.int32)

    x_give = take_half(1 - core_ids, hbm(x))
    x, x_give = lax.optimization_barrier((x, x_give))
    x_got = lax.ppermute(x_give, "narrow", swap)

    order = wave_perm.reshape(wide, ring, 2, slots).transpose(1, 2, 3, 0)
    order = jnp.concatenate([order, order], axis=0)
    order = jnp.concatenate([order, order[:, :1]], axis=1)
    order = lax.dynamic_slice(order, (y, core, 0, 0), (ring, 2, slots, wide))[:, :, :, None]
    columns = (ring, 2, slots, 2, wide)
    wave = jnp.broadcast_to(order, columns).reshape(-1).astype(F32)
    shift = jnp.tile(jnp.repeat(jnp.array([0.0, 640.0], F32), wide), ring * 2 * slots)
    lons = jnp.arange(2 * lon, dtype=jnp.int32) % lon
    side = jnp.arange(2 * lon, dtype=jnp.int32) // lon
    lons = (lons + lon * jnp.where(side == 0, v, v ^ 1)).astype(F32)

    def table(columns):
        return cosine_of_phase(wave[columns][:, None] * lons[None, :] - shift[columns][:, None])

    def table_t(rows):
        return cosine_of_phase(wave[None, :] * lons[rows][:, None] - shift[None, :])

    blocks = interp_weights.shape[0]
    contrib = jnp.einsum(
        "bai,bac->bic", interp_weights, x.reshape(blocks, BS, channels), preferred_element_type=F32
    ).astype(BF)
    owner = depart_owner[:, 0]
    ids = jnp.arange(blocks, dtype=jnp.int32)
    rank = jnp.sum(
        ((owner[:, None] == owner[None, :]) & (ids[None, :] < ids[:, None])).astype(jnp.int32), axis=1
    )
    slot = owner * CAP + rank
    pick = jnp.arange(wide * CAP, dtype=jnp.int32)[:, None] == slot[None, :]
    target = jnp.max(jnp.where(pick, depart_block[None, :], -1), axis=1)
    cut = [0]
    for n in COUNTS:
        cut.append(cut[-1] + n)

    def send_deposit(piece):
        out = lax.all_to_all(
            piece.reshape(wide, -1, channels), "wide", split_axis=0, concat_axis=0, tiled=True
        )
        return out.reshape(-1, BS, channels)

    piece_1 = pack(owner, rank, contrib, wide, cut[0], COUNTS[0])
    got_1 = send_deposit(piece_1)

    per = 256
    x_late, piece_1 = lax.optimization_barrier((x, piece_1))
    x = x_late
    far_a, far_b = dft(core_ids, table(slice(2 * per, 3 * per)), x, x_got, 4)

    near = jnp.concatenate([wave[3 * per :], wave[: 2 * per]])
    near_shift = jnp.concatenate([shift[3 * per :], shift[: 2 * per]])
    near = cosine_of_phase(near[:, None] * lons[None, :] - near_shift[:, None])
    down_a, down_b, own_a, own_b, up_a, up_b = dft(core_ids, near, x, x_got, 4)

    relay_a = lax.ppermute(far_a, "narrow", up)
    relay_b = lax.ppermute(far_b, "narrow", down)
    direct_b = lax.ppermute(up_b, "narrow", up)
    direct_a = lax.ppermute(down_a, "narrow", down)
    sum_a = lax.ppermute((relay_a.astype(F32) + up_a.astype(F32)).astype(BF), "narrow", up)
    sum_b = lax.ppermute((relay_b.astype(F32) + down_b.astype(F32)).astype(BF), "narrow", down)
    marks = jnp.pad(
        target.reshape(wide, 1, CAP).astype(BF), ((0, 0), (0, lat - 1), (0, 128 - CAP))
    )
    slot_waves = lax.dynamic_slice(wave_perm, ((w * narrow + v) * slots,), (slots,))
    mode_ids = jnp.concatenate([core_ids, slot_waves])
    proj, back = mode_proj.astype(BF), mode_back.astype(BF)
    piece_2 = pack(owner, rank, contrib, wide, cut[1], COUNTS[1])
    own_a, piece_2, proj, back, marks = lax.optimization_barrier(
        (own_a, piece_2, proj, back, marks)
    )
    rows, other = to_rows([own_a, sum_a, direct_a, own_b, sum_b, direct_b], marks, wide)
    rows = join(rows, vmem(lax.ppermute(other, "narrow", swap)))
    rows, got_1 = lax.optimization_barrier((rows, got_1))
    rows = lax.all_to_all(rows, "wide", split_axis=0, concat_axis=0, tiled=True)
    targets = rows[:, 0, 4 * channels : 4 * channels + CAP].astype(jnp.int32)
    lists = [
        by_latitude(targets[:, i:j].reshape(-1), lat, lon // BS) for i, j in zip(cut, cut[1:])
    ]
    synth = modes(
        mode_ids, rows.reshape(lat_total, -1), hbm(legendre), vmem(proj), vmem(back),
        mode_depth.reshape(1, -1), wide, lat,
    )
    synth = lax.all_to_all(synth, "wide", split_axis=0, concat_axis=0, tiled=True)
    piece_2, synth = lax.optimization_barrier((piece_2, synth))
    got_2 = send_deposit(piece_2)

    own = to_columns(synth, lax.ppermute(synth[:, 1], "narrow", swap))
    below = lax.ppermute(own, "narrow", up)
    above = lax.ppermute(own, "narrow", down)
    across_a = lax.ppermute(below[0], "narrow", up)
    across_b = lax.ppermute(above[1], "narrow", down)
    pieces = [own, above, across_a, across_b, below]
    wave_got = lax.ppermute(idft(table_t(slice(lon, 2 * lon)), *pieces, 4), "narrow", swap)
    wave_own = idft(table_t(slice(0, lon)), *pieces, 4)
    begun = base(core_ids, wave_own, wave_got, lists[0], got_1)
    return finish(begun, lists[1], hbm(got_2))


def solution(mesh):
    in_specs = (
        P("wide", "narrow", None),
        P(("wide", "narrow"), None, None),
        P(("wide", "narrow"), None),
        P(("wide", "narrow")),
        P(),
        P(("wide", "narrow"), None, None),
        P(),
        P(),
        P(),
    )
    out_specs = P("wide", "narrow", None)
    return jax.shard_map(shards, mesh=mesh, in_specs=in_specs, out_specs=out_specs, check_vma=False)
```

```python
import math

import numpy as np
import jax
import jax.numpy as jnp
from jax import lax
from jax.experimental import pallas as pl
from jax.experimental.pallas import tpu as pltpu
from jax.sharding import PartitionSpec as P

NLON = 2560
BS = 32
CAP = 5
COUNTS = (2, 3)
BF = jnp.bfloat16
F32 = jnp.float32


def _half_sine_coefficients():
    nodes = (np.cos(np.pi * (np.arange(64) + 0.5) / 64) + 1) * 0.5 * (np.pi / 2) ** 2
    root = np.sqrt(nodes)
    return [float(c) for c in np.polynomial.polynomial.polyfit(nodes, np.sin(root) / root, 5)]


SINE = _half_sine_coefficients()


def cosine_of_phase(phase):
    turns = jnp.round(phase * (1.0 / NLON))
    u = (phase - turns * NLON) * (math.pi / NLON)
    z = u * u
    poly = jnp.full_like(z, SINE[-1])
    for coefficient in SINE[-2::-1]:
        poly = poly * z + coefficient
    s = u * poly
    return (1.0 - 2.0 * s * s).astype(BF)


def hbm(value):
    return pltpu.with_memory_space_constraint(value, pltpu.HBM)


def vmem(value):
    return pltpu.with_memory_space_constraint(value, pltpu.VMEM)


def take_half(side, x):
    lat, lon, channels = x.shape
    half = channels // 2

    def body(side_ref, x_hbm, o_ref, sem):
        lanes = pl.ds(pl.multiple_of(side_ref[0] * half, half), half)
        copies = [
            pltpu.make_async_copy(x_hbm.at[i, :, lanes], o_ref.at[i], sem.at[i]) for i in range(lat)
        ]
        for c in copies:
            c.start()
        for c in copies:
            c.wait()

    return pl.pallas_call(
        body,
        out_shape=pltpu.VMEM((lat, lon, half), BF),
        grid_spec=pltpu.PrefetchScalarGridSpec(
            num_scalar_prefetch=1,
            grid=(),
            in_specs=[pl.BlockSpec(memory_space=pl.ANY)],
            out_specs=pl.BlockSpec(memory_space=pltpu.VMEM),
            scratch_shapes=[pltpu.SemaphoreType.DMA((lat,))],
        ),
        name="take_half",
    )(side, x)


def dft_body(core_ref, t_ref, own_ref, got_ref, *outs):
    for lat in range(own_ref.shape[0]):
        x = jnp.concatenate([own_ref[lat], got_ref[lat]], axis=0)
        r = jnp.dot(t_ref[...], x, preferred_element_type=F32)
        for i, o in enumerate(outs):
            o[lat] = r[128 * i : 128 * i + 128].astype(BF)


def dft(core, table, x, got, step):
    rows = table.shape[0]
    lat, lon, channels = x.shape
    half = channels // 2
    n = rows // 128
    return pl.pallas_call(
        dft_body,
        out_shape=[jax.ShapeDtypeStruct((lat, 128, half), BF)] * n,
        grid_spec=pltpu.PrefetchScalarGridSpec(
            num_scalar_prefetch=1,
            grid=(lat // step,),
            in_specs=[
                pl.BlockSpec((rows, 2 * lon), lambda i, c: (0, 0)),
                pl.BlockSpec((step, lon, half), lambda i, c: (i, 0, c[0])),
                pl.BlockSpec((step, lon, half), lambda i, c: (i, 0, 0)),
            ],
            out_specs=[pl.BlockSpec((step, 128, half), lambda i, c: (i, 0, 0))] * n,
        ),
        compiler_params=pltpu.CompilerParams(vmem_limit_bytes=48 << 20),
        name="dft",
    )(core, table, x, got)


def rows_body(own_a, sum_a, direct_a, own_b, sum_b, direct_b, marks, o_hbm, o_other, o_mine, tmp, sem):
    wide, lat, width = o_mine.shape
    copies = [
        pltpu.make_async_copy(marks, o_hbm.at[:, :, pl.ds(2 * width, 128)], sem.at[0]),
        pltpu.make_async_copy(o_mine, o_hbm.at[:, :, pl.ds(0, width)], sem.at[1]),
    ]
    copies[0].start()
    half = own_a.shape[2]
    for s, parts in enumerate(((own_a, sum_a, direct_a), (own_b, sum_b, direct_b))):
        for q in range(4):
            for h in range(half // 128):
                t = tmp.at[(q * (half // 128) + h) % 4]
                lanes = slice(128 * h, 128 * h + 128)
                for l in range(lat):
                    value = sum(p[l, wide * q : wide * q + wide, lanes].astype(F32) for p in parts)
                    value = value * NLON ** (-0.5)
                    for j in range(wide // 8):
                        t[pl.ds(lat * 8 * j + l, 8, stride=lat), :] = value[8 * j : 8 * j + 8]
                col = q * half + 128 * h
                o_ref = (o_mine, o_other)[s]
                o_ref[:, :, col : col + 128] = t[...].astype(BF).reshape(wide, lat, 128)
        if s == 0:
            copies[1].start()
    for c in copies:
        c.wait()


def to_rows(pieces, marks, wide):
    lat, _, half = pieces[0].shape
    part = jax.ShapeDtypeStruct((wide, lat, 4 * half), BF)
    whole = pltpu.HBM((wide, lat, 8 * half + 128), BF)
    near, free = pl.BlockSpec(memory_space=pltpu.VMEM), pl.BlockSpec(memory_space=pl.ANY)
    return pl.pallas_call(
        rows_body,
        out_shape=[whole, part],
        in_specs=[near] * 7,
        out_specs=[free, near],
        scratch_shapes=[
            pltpu.VMEM(part.shape, BF),
            pltpu.VMEM((4, wide * lat, 128), F32),
            pltpu.SemaphoreType.DMA((2,)),
        ],
        compiler_params=pltpu.CompilerParams(vmem_limit_bytes=48 << 20),
        name="to_rows",
    )(*pieces, marks)


def join_body(rows_ref, got_ref, o_ref, sem):
    wide, _, width = got_ref.shape
    part = wide // 4
    copies = [
        pltpu.make_async_copy(
            got_ref.at[pl.ds(part * i, part)],
            o_ref.at[pl.ds(part * i, part), :, pl.ds(width, width)],
            sem.at[i],
        )
        for i in range(4)
    ]
    for c in copies:
        c.start()
    for c in copies:
        c.wait()


def join(rows, got):
    free = pl.BlockSpec(memory_space=pl.ANY)
    return pl.pallas_call(
        join_body,
        out_shape=pltpu.HBM(rows.shape, BF),
        in_specs=[free, pl.BlockSpec(memory_space=pltpu.VMEM)],
        out_specs=free,
        input_output_aliases={0: 0},
        scratch_shapes=[pltpu.SemaphoreType.DMA((4,))],
        name="join",
    )(rows, got)


def modes_body(ids_ref, fa_ref, fb_ref, fc_ref, fd_ref, leg_ref, p0_ref, p1_ref, b0_ref, b1_ref, depth_ref, o_ref, damp_ref):
    half = fa_ref.shape[1]
    degrees = leg_ref.shape[2]

    @pl.when(pl.program_id(0) == 0)
    def _():
        n = lax.broadcasted_iota(jnp.int32, damp_ref.shape, 0).astype(F32)
        damp_ref[...] = 1.0 / (1.0 + n * (n + 1.0) * depth_ref[...])

    degree = lax.broadcasted_iota(jnp.int32, leg_ref.shape[1:], 1)
    leg = leg_ref[0].astype(F32)
    leg = jnp.where(degree >= ids_ref[1 + pl.program_id(0)], leg, jnp.zeros_like(leg))
    turned = leg.T.astype(BF)
    leg = leg.astype(BF)
    spectra = [
        jnp.dot(turned, f[...], preferred_element_type=F32).astype(BF)
        for f in (fa_ref, fb_ref, fc_ref, fd_ref)
    ]
    low = jnp.concatenate([spectra[0], spectra[2]], axis=0)
    high = jnp.concatenate([spectra[1], spectra[3]], axis=0)
    modal = jnp.dot(low, p0_ref[...], preferred_element_type=F32)
    modal += jnp.dot(high, p1_ref[...], preferred_element_type=F32)
    modal = jnp.concatenate(
        [(modal[degrees * p : degrees * p + degrees] * damp_ref[...]).astype(BF) for p in range(2)], axis=0
    )
    wide, _, lat, _ = o_ref.shape
    for i, b_ref in enumerate((b0_ref, b1_ref)):
        back = jnp.dot(modal, b_ref[...], preferred_element_type=F32).astype(BF)
        for p in range(2):
            synth = jnp.dot(leg, back[degrees * p : degrees * p + degrees], preferred_element_type=F32)
            o_ref[:, i, :, half * p : half * p + half] = synth.astype(BF).reshape(wide, lat, half)


def modes(ids, f, legendre, proj, back, depth, wide, lat):
    slots, total, degrees = legendre.shape
    channels = proj.shape[0]
    half = channels // 2
    part = [pl.BlockSpec((total, half), lambda k, c, j=j: (0, j + 2 * k)) for j in (0, 4, 1, 5)]
    return pl.pallas_call(
        modes_body,
        out_shape=jax.ShapeDtypeStruct((wide, 2, lat, 4 * half), BF),
        grid_spec=pltpu.PrefetchScalarGridSpec(
            num_scalar_prefetch=1,
            grid=(slots,),
            in_specs=part
            + [
                pl.BlockSpec((1, total, degrees), lambda k, c: (k, 0, 0)),
                pl.BlockSpec((half, channels), lambda k, c: (c[0], 0)),
                pl.BlockSpec((half, channels), lambda k, c: (1 - c[0], 0)),
                pl.BlockSpec((channels, half), lambda k, c: (0, c[0])),
                pl.BlockSpec((channels, half), lambda k, c: (0, 1 - c[0])),
                pl.BlockSpec((1, channels), lambda k, c: (0, 0)),
            ],
            out_specs=pl.BlockSpec((wide, 2, lat, 2 * half), lambda k, c: (0, 0, 0, k)),
            scratch_shapes=[pltpu.VMEM((degrees, channels), F32)],
        ),
        compiler_params=pltpu.CompilerParams(vmem_limit_bytes=48 << 20),
        name="modes",
    )(ids, f, f, f, f, legendre, proj, proj, back, back, depth)


def columns_body(keep, take, o_ref, tmp):
    wide, lat, _ = take.shape
    half = o_ref.shape[3]
    for s, src in enumerate((keep, take)):
        for q in range(4):
            for h in range(half // 128):
                t = tmp.at[(q * (half // 128) + h) % 4]
                col = slice(half * q + 128 * h, half * q + 128 * h + 128)
                value = src[:, 0, :, col] if s == 0 else src[:, :, col]
                t[...] = value.astype(F32).reshape(wide * lat, 128)
                for l in range(lat):
                    rows = [t[pl.ds(lat * 8 * j + l, 8, stride=lat), :] for j in range(wide // 8)]
                    rows = jnp.concatenate(rows, axis=0).astype(BF)
                    o_ref[s, l, wide * q : wide * q + wide, 128 * h : 128 * h + 128] = rows


def to_columns(keep, take):
    wide, lat, width = take.shape
    half = width // 4
    return pl.pallas_call(
        columns_body,
        out_shape=jax.ShapeDtypeStruct((2, lat, 4 * wide, half), BF),
        grid=(1,),
        in_specs=[
            pl.BlockSpec((wide, 1, lat, width), lambda i: (0, 0, 0, 0)),
            pl.BlockSpec((wide, lat, width), lambda i: (0, 0, 0)),
        ],
        out_specs=pl.BlockSpec((2, lat, 4 * wide, half), lambda i: (0, 0, 0, 0)),
        scratch_shapes=[pltpu.VMEM((4, wide * lat, 128), F32)],
        compiler_params=pltpu.CompilerParams(vmem_limit_bytes=48 << 20),
        name="to_columns",
    )(keep, take)


def idft_body(t_ref, own, above, across_a, across_b, below, o_ref):
    for lat in range(o_ref.shape[0]):
        g = [own[0, lat], own[1, lat], above[0, lat], above[1, lat]]
        g += [across_a[lat], across_b[lat], below[0, lat], below[1, lat]]
        r = jnp.dot(t_ref[...], jnp.concatenate(g, axis=0), preferred_element_type=F32)
        o_ref[lat] = (r * NLON ** (-0.5)).astype(BF)


def idft(table, own, above, across_a, across_b, below, step):
    _, lat, rows, half = own.shape
    lon = table.shape[0]
    pair = pl.BlockSpec((2, step, rows, half), lambda i: (0, i, 0, 0))
    single = pl.BlockSpec((step, rows, half), lambda i: (i, 0, 0))
    return pl.pallas_call(
        idft_body,
        out_shape=jax.ShapeDtypeStruct((lat, lon, half), BF),
        grid=(lat // step,),
        in_specs=[pl.BlockSpec(table.shape, lambda i: (0, 0)), pair, pair, single, single, pair],
        out_specs=pl.BlockSpec((step, lon, half), lambda i: (i, 0, 0)),
        compiler_params=pltpu.CompilerParams(vmem_limit_bytes=48 << 20),
        name="idft",
    )(table, own, above, across_a, across_b, below)


def pack(owner, rank, contrib, owners, first, count):
    blocks, rows, channels = contrib.shape

    def body(owner_ref, rank_ref, contrib_ref, o_hbm, sem):
        def each(b, act):
            r = rank_ref[b] - first

            @pl.when((r >= 0) & (r < count))
            def _():
                act(pltpu.make_async_copy(contrib_ref.at[b], o_hbm.at[owner_ref[b], r], sem.at[b]))

            return 0

        lax.fori_loop(0, blocks, lambda b, _: each(b, lambda c: c.start()), 0)
        lax.fori_loop(0, blocks, lambda b, _: each(b, lambda c: c.wait()), 0)

    return pl.pallas_call(
        body,
        out_shape=pltpu.HBM((owners, count, rows, channels), BF),
        grid_spec=pltpu.PrefetchScalarGridSpec(
            num_scalar_prefetch=2,
            grid=(),
            in_specs=[pl.BlockSpec(memory_space=pltpu.VMEM)],
            out_specs=pl.BlockSpec(memory_space=pl.ANY),
            scratch_shapes=[pltpu.SemaphoreType.DMA((blocks,))],
        ),
        compiler_params=pltpu.CompilerParams(vmem_limit_bytes=48 << 20),
        name="pack",
    )(owner, rank, vmem(contrib))


def add_blocks(i, start, order, target, piece, out, blocks):
    def step(e, _):
        s = order[e]
        rows = pl.ds(pl.multiple_of((target[s] - i * blocks) * BS, BS), BS)
        out[i, rows, :] = out[i, rows, :] + piece[s].astype(F32)
        return 0

    lax.fori_loop(start[i], start[i + 1], step, 0)


def base(core, own, got, lists, piece):
    lat, lon, half = own.shape

    def body(core_ref, start, order, target, own_ref, got_ref, piece_ref, o_ref):
        mine = pl.ds(pl.multiple_of(core_ref[0] * half, half), half)
        other = pl.ds(pl.multiple_of((1 - core_ref[0]) * half, half), half)

        def latitude(i, _):
            o_ref[i, :, mine] = own_ref[i].astype(F32)
            o_ref[i, :, other] = got_ref[i].astype(F32)
            add_blocks(i, start, order, target, piece_ref, o_ref, lon // BS)
            return 0

        lax.fori_loop(0, lat, latitude, 0)

    return pl.pallas_call(
        body,
        out_shape=pltpu.HBM((lat, lon, 2 * half), F32),
        grid_spec=pltpu.PrefetchScalarGridSpec(
            num_scalar_prefetch=4,
            grid=(),
            in_specs=[pl.BlockSpec(memory_space=pltpu.VMEM)] * 3,
            out_specs=pl.BlockSpec(memory_space=pltpu.VMEM),
        ),
        compiler_params=pltpu.CompilerParams(vmem_limit_bytes=48 << 20),
        name="base",
    )(core, *lists, own, got, piece)


def finish(begun, lists, piece):
    slots, rows, channels = piece.shape
    blocks = begun.shape[0]

    def body(start, order, target, begun_hbm, piece_hbm, o_hbm, acc, recv, read_sem, recv_sem, write_sem):
        first = start[0]

        def entry(e):
            t = target[order[e]]
            opens = (e == first) | (target[order[jnp.maximum(e - 1, 0)]] != t)
            closes = (e == slots - 1) | (target[order[jnp.minimum(e + 1, slots - 1)]] != t)
            return t, opens, closes

        def read(t):
            return pltpu.make_async_copy(begun_hbm.at[t], acc.at[t], read_sem.at[t])

        def write(t):
            return pltpu.make_async_copy(acc.at[t], o_hbm.at[t], write_sem.at[t])

        def arrive(e):
            return pltpu.make_async_copy(piece_hbm.at[order[e]], recv.at[e], recv_sem.at[e])

        def load(e, _):
            t, opens, _ = entry(e)
            arrive(e).start()
            pl.when(opens)(lambda: read(t).start())
            return 0

        def add(e, _):
            t, opens, closes = entry(e)
            pl.when(opens)(lambda: read(t).wait())
            arrive(e).wait()
            acc[t] = acc[t] + recv[e].astype(F32)
            pl.when(closes)(lambda: write(t).start())
            return 0

        def drain(e, _):
            t, _, closes = entry(e)
            pl.when(closes)(lambda: write(t).wait())
            return 0

        for step in (load, add, drain):
            lax.fori_loop(first, slots, step, 0)

    return pl.pallas_call(
        body,
        out_shape=pltpu.HBM(begun.shape, F32),
        grid_spec=pltpu.PrefetchScalarGridSpec(
            num_scalar_prefetch=3,
            grid=(),
            in_specs=[pl.BlockSpec(memory_space=pl.ANY)] * 2,
            out_specs=pl.BlockSpec(memory_space=pl.ANY),
            scratch_shapes=[
                pltpu.VMEM(begun.shape, F32),
                pltpu.VMEM(piece.shape, BF),
                pltpu.SemaphoreType.DMA((blocks,)),
                pltpu.SemaphoreType.DMA((slots,)),
                pltpu.SemaphoreType.DMA((blocks,)),
            ],
        ),
        input_output_aliases={3: 0},
        compiler_params=pltpu.CompilerParams(vmem_limit_bytes=48 << 20),
        name="finish",
    )(*lists, begun, piece)


def by_latitude(target, lat, blocks):
    ids = jnp.arange(target.shape[0], dtype=jnp.int32)
    before = (target[None, :] < target[:, None]) | (
        (target[None, :] == target[:, None]) & (ids[None, :] < ids[:, None])
    )
    place = jnp.sum(before.astype(jnp.int32), axis=1)
    order = jnp.sum(jnp.where(place[None, :] == ids[:, None], ids[None, :], 0), axis=1)
    first = jnp.arange(lat + 1, dtype=jnp.int32) * blocks
    start = jnp.sum((target[None, :] < first[:, None]).astype(jnp.int32), axis=1)
    return start, order, target


def shards(
    grid_adjoint_fields,
    interp_weights,
    depart_owner,
    depart_block,
    wave_perm,
    legendre,
    mode_proj,
    mode_back,
    mode_depth,
):
    x = grid_adjoint_fields
    wide = lax.axis_size("wide")
    narrow = lax.axis_size("narrow")
    w = lax.axis_index("wide")
    v = lax.axis_index("narrow")
    y, core = v // 2, v % 2
    ring = narrow // 2
    lat, lon, channels = x.shape
    half = channels // 2
    slots, lat_total, degrees = legendre.shape
    swap = [(i, i ^ 1) for i in range(narrow)]
    up = [(i, (i + 2) % narrow) for i in range(narrow)]
    down = [(i, (i - 2) % narrow) for i in range(narrow)]
    core_ids = core[None].astype(jnp.int32)

    x_give = take_half(1 - core_ids, hbm(x))
    x, x_give = lax.optimization_barrier((x, x_give))
    x_got = lax.ppermute(x_give, "narrow", swap)

    order = wave_perm.reshape(wide, ring, 2, slots).transpose(1, 2, 3, 0)
    order = jnp.concatenate([order, order], axis=0)
    order = jnp.concatenate([order, order[:, :1]], axis=1)
    order = lax.dynamic_slice(order, (y, core, 0, 0), (ring, 2, slots, wide))[:, :, :, None]
    columns = (ring, 2, slots, 2, wide)
    wave = jnp.broadcast_to(order, columns).reshape(-1).astype(F32)
    shift = jnp.tile(jnp.repeat(jnp.array([0.0, 640.0], F32), wide), ring * 2 * slots)
    lons = jnp.arange(2 * lon, dtype=jnp.int32) % lon
    side = jnp.arange(2 * lon, dtype=jnp.int32) // lon
    lons = (lons + lon * jnp.where(side == 0, v, v ^ 1)).astype(F32)

    def table(columns):
        return cosine_of_phase(wave[columns][:, None] * lons[None, :] - shift[columns][:, None])

    def table_t(rows):
        return cosine_of_phase(wave[None, :] * lons[rows][:, None] - shift[None, :])

    blocks = interp_weights.shape[0]
    contrib = jnp.einsum(
        "bai,bac->bic", interp_weights, x.reshape(blocks, BS, channels), preferred_element_type=F32
    ).astype(BF)
    owner = depart_owner[:, 0]
    ids = jnp.arange(blocks, dtype=jnp.int32)
    rank = jnp.sum(
        ((owner[:, None] == owner[None, :]) & (ids[None, :] < ids[:, None])).astype(jnp.int32), axis=1
    )
    slot = owner * CAP + rank
    pick = jnp.arange(wide * CAP, dtype=jnp.int32)[:, None] == slot[None, :]
    target = jnp.max(jnp.where(pick, depart_block[None, :], -1), axis=1)
    cut = [0]
    for n in COUNTS:
        cut.append(cut[-1] + n)

    def send_deposit(piece):
        out = lax.all_to_all(
            piece.reshape(wide, -1, channels), "wide", split_axis=0, concat_axis=0, tiled=True
        )
        return out.reshape(-1, BS, channels)

    piece_1 = pack(owner, rank, contrib, wide, cut[0], COUNTS[0])
    got_1 = send_deposit(piece_1)

    per = 256
    x_late, piece_1 = lax.optimization_barrier((x, piece_1))
    x = x_late
    far_a, far_b = dft(core_ids, table(slice(2 * per, 3 * per)), x, x_got, 4)

    near = jnp.concatenate([wave[3 * per :], wave[: 2 * per]])
    near_shift = jnp.concatenate([shift[3 * per :], shift[: 2 * per]])
    near = cosine_of_phase(near[:, None] * lons[None, :] - near_shift[:, None])
    down_a, down_b, own_a, own_b, up_a, up_b = dft(core_ids, near, x, x_got, 4)

    relay_a = lax.ppermute(far_a, "narrow", up)
    relay_b = lax.ppermute(far_b, "narrow", down)
    direct_b = lax.ppermute(up_b, "narrow", up)
    direct_a = lax.ppermute(down_a, "narrow", down)
    sum_a = lax.ppermute((relay_a.astype(F32) + up_a.astype(F32)).astype(BF), "narrow", up)
    sum_b = lax.ppermute((relay_b.astype(F32) + down_b.astype(F32)).astype(BF), "narrow", down)
    marks = jnp.pad(
        target.reshape(wide, 1, CAP).astype(BF), ((0, 0), (0, lat - 1), (0, 128 - CAP))
    )
    slot_waves = lax.dynamic_slice(wave_perm, ((w * narrow + v) * slots,), (slots,))
    mode_ids = jnp.concatenate([core_ids, slot_waves])
    proj, back = mode_proj.astype(BF), mode_back.astype(BF)
    piece_2 = pack(owner, rank, contrib, wide, cut[1], COUNTS[1])
    own_a, piece_2, proj, back, marks = lax.optimization_barrier(
        (own_a, piece_2, proj, back, marks)
    )
    rows, other = to_rows([own_a, sum_a, direct_a, own_b, sum_b, direct_b], marks, wide)
    rows = join(rows, vmem(lax.ppermute(other, "narrow", swap)))
    rows, got_1 = lax.optimization_barrier((rows, got_1))
    rows = lax.all_to_all(rows, "wide", split_axis=0, concat_axis=0, tiled=True)
    targets = rows[:, 0, 4 * channels : 4 * channels + CAP].astype(jnp.int32)
    lists = [
        by_latitude(targets[:, i:j].reshape(-1), lat, lon // BS) for i, j in zip(cut, cut[1:])
    ]
    synth = modes(
        mode_ids, rows.reshape(lat_total, -1), hbm(legendre), vmem(proj), vmem(back),
        mode_depth.reshape(1, -1), wide, lat,
    )
    synth = lax.all_to_all(synth, "wide", split_axis=0, concat_axis=0, tiled=True)
    piece_2, synth = lax.optimization_barrier((piece_2, synth))
    got_2 = send_deposit(piece_2)

    own = to_columns(synth, lax.ppermute(synth[:, 1], "narrow", swap))
    below = lax.ppermute(own, "narrow", up)
    above = lax.ppermute(own, "narrow", down)
    across_a = lax.ppermute(below[0], "narrow", up)
    across_b = lax.ppermute(above[1], "narrow", down)
    pieces = [own, above, across_a, across_b, below]
    wave_got = lax.ppermute(idft(table_t(slice(lon, 2 * lon)), *pieces, 4), "narrow", swap)
    wave_own = idft(table_t(slice(0, lon)), *pieces, 4)
    begun = base(core_ids, wave_own, wave_got, lists[0], got_1)
    begun = begun.reshape(blocks, BS, channels)
    return finish(begun, lists[1], hbm(got_2)).reshape(lat, lon, channels)


def solution(mesh):
    in_specs = (
        P("wide", "narrow", None),
        P(("wide", "narrow"), None, None),
        P(("wide", "narrow"), None),
        P(("wide", "narrow")),
        P(),
        P(("wide", "narrow"), None, None),
        P(),
        P(),
        P(),
    )
    out_specs = P("wide", "narrow", None)
    return jax.shard_map(shards, mesh=mesh, in_specs=in_specs, out_specs=out_specs, check_vma=False)
```

```python
import math

import numpy as np
import jax
import jax.numpy as jnp
from jax import lax
from jax.experimental import pallas as pl
from jax.experimental.pallas import tpu as pltpu
from jax.sharding import PartitionSpec as P

NLON = 2560
BS = 32
CAP = 5
COUNTS = (2, 3)
BF = jnp.bfloat16
F32 = jnp.float32


def _half_sine_coefficients():
    nodes = (np.cos(np.pi * (np.arange(64) + 0.5) / 64) + 1) * 0.5 * (np.pi / 2) ** 2
    root = np.sqrt(nodes)
    return [float(c) for c in np.polynomial.polynomial.polyfit(nodes, np.sin(root) / root, 5)]


SINE = _half_sine_coefficients()


def cosine_of_phase(phase):
    turns = jnp.round(phase * (1.0 / NLON))
    u = (phase - turns * NLON) * (math.pi / NLON)
    z = u * u
    poly = jnp.full_like(z, SINE[-1])
    for coefficient in SINE[-2::-1]:
        poly = poly * z + coefficient
    s = u * poly
    return (1.0 - 2.0 * s * s).astype(BF)


def hbm(value):
    return pltpu.with_memory_space_constraint(value, pltpu.HBM)


def vmem(value):
    return pltpu.with_memory_space_constraint(value, pltpu.VMEM)


def half_body(side_ref, x_ref, o_ref):
    o_ref[...] = x_ref[...]


def take_half(side, x):
    lat, lon, channels = x.shape
    half = channels // 2
    step = lat // 2
    return pl.pallas_call(
        half_body,
        out_shape=jax.ShapeDtypeStruct((lat, lon, half), BF),
        grid_spec=pltpu.PrefetchScalarGridSpec(
            num_scalar_prefetch=1,
            grid=(lat // step,),
            in_specs=[pl.BlockSpec((step, lon, half), lambda i, c: (i, 0, c[0]))],
            out_specs=pl.BlockSpec((step, lon, half), lambda i, c: (i, 0, 0)),
        ),
        name="take_half",
    )(side, x)


def dft_body(core_ref, t_ref, own_ref, got_ref, *outs):
    for lat in range(own_ref.shape[0]):
        x = jnp.concatenate([own_ref[lat], got_ref[lat]], axis=0)
        r = jnp.dot(t_ref[...], x, preferred_element_type=F32)
        for i, o in enumerate(outs):
            o[lat] = r[128 * i : 128 * i + 128].astype(BF)


def dft(core, table, x, got, step):
    rows = table.shape[0]
    lat, lon, channels = x.shape
    half = channels // 2
    n = rows // 128
    return pl.pallas_call(
        dft_body,
        out_shape=[jax.ShapeDtypeStruct((lat, 128, half), BF)] * n,
        grid_spec=pltpu.PrefetchScalarGridSpec(
            num_scalar_prefetch=1,
            grid=(lat // step,),
            in_specs=[
                pl.BlockSpec((rows, 2 * lon), lambda i, c: (0, 0)),
                pl.BlockSpec((step, lon, half), lambda i, c: (i, 0, c[0])),
                pl.BlockSpec((step, lon, half), lambda i, c: (i, 0, 0)),
            ],
            out_specs=[pl.BlockSpec((step, 128, half), lambda i, c: (i, 0, 0))] * n,
        ),
        compiler_params=pltpu.CompilerParams(vmem_limit_bytes=48 << 20),
        name="dft",
    )(core, table, x, got)


def rows_body(own_a, sum_a, direct_a, own_b, sum_b, direct_b, marks, o_hbm, o_other, o_mine, tmp, sem):
    wide, lat, width = o_mine.shape
    copies = [
        pltpu.make_async_copy(marks, o_hbm.at[:, :, pl.ds(2 * width, 128)], sem.at[0]),
        pltpu.make_async_copy(o_mine, o_hbm.at[:, :, pl.ds(0, width)], sem.at[1]),
    ]
    copies[0].start()
    half = own_a.shape[2]
    for s, parts in enumerate(((own_a, sum_a, direct_a), (own_b, sum_b, direct_b))):
        for q in range(4):
            for h in range(half // 128):
                t = tmp.at[(q * (half // 128) + h) % 4]
                lanes = slice(128 * h, 128 * h + 128)
                for l in range(lat):
                    value = sum(p[l, wide * q : wide * q + wide, lanes].astype(F32) for p in parts)
                    value = value * NLON ** (-0.5)
                    for j in range(wide // 8):
                        t[pl.ds(lat * 8 * j + l, 8, stride=lat), :] = value[8 * j : 8 * j + 8]
                col = q * half + 128 * h
                o_ref = (o_mine, o_other)[s]
                o_ref[:, :, col : col + 128] = t[...].astype(BF).reshape(wide, lat, 128)
        if s == 0:
            copies[1].start()
    for c in copies:
        c.wait()


def to_rows(pieces, marks, wide):
    lat, _, half = pieces[0].shape
    part = jax.ShapeDtypeStruct((wide, lat, 4 * half), BF)
    whole = pltpu.HBM((wide, lat, 8 * half + 128), BF)
    near, free = pl.BlockSpec(memory_space=pltpu.VMEM), pl.BlockSpec(memory_space=pl.ANY)
    return pl.pallas_call(
        rows_body,
        out_shape=[whole, part],
        in_specs=[near] * 7,
        out_specs=[free, near],
        scratch_shapes=[
            pltpu.VMEM(part.shape, BF),
            pltpu.VMEM((4, wide * lat, 128), F32),
            pltpu.SemaphoreType.DMA((2,)),
        ],
        compiler_params=pltpu.CompilerParams(vmem_limit_bytes=48 << 20),
        name="to_rows",
    )(*pieces, marks)


def join_body(rows_ref, got_ref, o_ref, sem):
    wide, _, width = got_ref.shape
    part = wide // 4
    copies = [
        pltpu.make_async_copy(
            got_ref.at[pl.ds(part * i, part)],
            o_ref.at[pl.ds(part * i, part), :, pl.ds(width, width)],
            sem.at[i],
        )
        for i in range(4)
    ]
    for c in copies:
        c.start()
    for c in copies:
        c.wait()


def join(rows, got):
    free = pl.BlockSpec(memory_space=pl.ANY)
    return pl.pallas_call(
        join_body,
        out_shape=pltpu.HBM(rows.shape, BF),
        in_specs=[free, pl.BlockSpec(memory_space=pltpu.VMEM)],
        out_specs=free,
        input_output_aliases={0: 0},
        scratch_shapes=[pltpu.SemaphoreType.DMA((4,))],
        name="join",
    )(rows, got)


def modes_body(ids_ref, fa_ref, fb_ref, fc_ref, fd_ref, leg_ref, p0_ref, p1_ref, b0_ref, b1_ref, depth_ref, o_ref, damp_ref):
    half = fa_ref.shape[1]
    degrees = leg_ref.shape[2]

    @pl.when(pl.program_id(0) == 0)
    def _():
        n = lax.broadcasted_iota(jnp.int32, damp_ref.shape, 0).astype(F32)
        damp_ref[...] = 1.0 / (1.0 + n * (n + 1.0) * depth_ref[...])

    degree = lax.broadcasted_iota(jnp.int32, leg_ref.shape[1:], 1)
    leg = leg_ref[0].astype(F32)
    leg = jnp.where(degree >= ids_ref[1 + pl.program_id(0)], leg, jnp.zeros_like(leg))
    turned = leg.T.astype(BF)
    leg = leg.astype(BF)
    spectra = [
        jnp.dot(turned, f[...], preferred_element_type=F32).astype(BF)
        for f in (fa_ref, fb_ref, fc_ref, fd_ref)
    ]
    low = jnp.concatenate([spectra[0], spectra[2]], axis=0)
    high = jnp.concatenate([spectra[1], spectra[3]], axis=0)
    modal = jnp.dot(low, p0_ref[...], preferred_element_type=F32)
    modal += jnp.dot(high, p1_ref[...], preferred_element_type=F32)
    modal = jnp.concatenate(
        [(modal[degrees * p : degrees * p + degrees] * damp_ref[...]).astype(BF) for p in range(2)], axis=0
    )
    wide, _, lat, _ = o_ref.shape
    for i, b_ref in enumerate((b0_ref, b1_ref)):
        back = jnp.dot(modal, b_ref[...], preferred_element_type=F32).astype(BF)
        for p in range(2):
            synth = jnp.dot(leg, back[degrees * p : degrees * p + degrees], preferred_element_type=F32)
            o_ref[:, i, :, half * p : half * p + half] = synth.astype(BF).reshape(wide, lat, half)


def modes(ids, f, legendre, proj, back, depth, wide, lat):
    slots, total, degrees = legendre.shape
    channels = proj.shape[0]
    half = channels // 2
    part = [pl.BlockSpec((total, half), lambda k, c, j=j: (0, j + 2 * k)) for j in (0, 4, 1, 5)]
    return pl.pallas_call(
        modes_body,
        out_shape=jax.ShapeDtypeStruct((wide, 2, lat, 4 * half), BF),
        grid_spec=pltpu.PrefetchScalarGridSpec(
            num_scalar_prefetch=1,
            grid=(slots,),
            in_specs=part
            + [
                pl.BlockSpec((1, total, degrees), lambda k, c: (k, 0, 0)),
                pl.BlockSpec((half, channels), lambda k, c: (c[0], 0)),
                pl.BlockSpec((half, channels), lambda k, c: (1 - c[0], 0)),
                pl.BlockSpec((channels, half), lambda k, c: (0, c[0])),
                pl.BlockSpec((channels, half), lambda k, c: (0, 1 - c[0])),
                pl.BlockSpec((1, channels), lambda k, c: (0, 0)),
            ],
            out_specs=pl.BlockSpec((wide, 2, lat, 2 * half), lambda k, c: (0, 0, 0, k)),
            scratch_shapes=[pltpu.VMEM((degrees, channels), F32)],
        ),
        compiler_params=pltpu.CompilerParams(vmem_limit_bytes=48 << 20),
        name="modes",
    )(ids, f, f, f, f, legendre, proj, proj, back, back, depth)


def columns_body(keep, take, o_ref, tmp):
    wide, lat, _ = take.shape
    half = o_ref.shape[3]
    for s, src in enumerate((keep, take)):
        for q in range(4):
            for h in range(half // 128):
                t = tmp.at[(q * (half // 128) + h) % 4]
                col = slice(half * q + 128 * h, half * q + 128 * h + 128)
                value = src[:, 0, :, col] if s == 0 else src[:, :, col]
                t[...] = value.astype(F32).reshape(wide * lat, 128)
                for l in range(lat):
                    rows = [t[pl.ds(lat * 8 * j + l, 8, stride=lat), :] for j in range(wide // 8)]
                    rows = jnp.concatenate(rows, axis=0).astype(BF)
                    o_ref[s, l, wide * q : wide * q + wide, 128 * h : 128 * h + 128] = rows


def to_columns(keep, take):
    wide, lat, width = take.shape
    half = width // 4
    return pl.pallas_call(
        columns_body,
        out_shape=jax.ShapeDtypeStruct((2, lat, 4 * wide, half), BF),
        grid=(1,),
        in_specs=[
            pl.BlockSpec((wide, 1, lat, width), lambda i: (0, 0, 0, 0)),
            pl.BlockSpec((wide, lat, width), lambda i: (0, 0, 0)),
        ],
        out_specs=pl.BlockSpec((2, lat, 4 * wide, half), lambda i: (0, 0, 0, 0)),
        scratch_shapes=[pltpu.VMEM((4, wide * lat, 128), F32)],
        compiler_params=pltpu.CompilerParams(vmem_limit_bytes=48 << 20),
        name="to_columns",
    )(keep, take)


def idft_body(t_ref, own, above, across_a, across_b, below, o_ref):
    for lat in range(o_ref.shape[0]):
        g = [own[0, lat], own[1, lat], above[0, lat], above[1, lat]]
        g += [across_a[lat], across_b[lat], below[0, lat], below[1, lat]]
        r = jnp.dot(t_ref[...], jnp.concatenate(g, axis=0), preferred_element_type=F32)
        o_ref[lat] = (r * NLON ** (-0.5)).astype(BF)


def idft(table, own, above, across_a, across_b, below, step):
    _, lat, rows, half = own.shape
    lon = table.shape[0]
    pair = pl.BlockSpec((2, step, rows, half), lambda i: (0, i, 0, 0))
    single = pl.BlockSpec((step, rows, half), lambda i: (i, 0, 0))
    return pl.pallas_call(
        idft_body,
        out_shape=jax.ShapeDtypeStruct((lat, lon, half), BF),
        grid=(lat // step,),
        in_specs=[pl.BlockSpec(table.shape, lambda i: (0, 0)), pair, pair, single, single, pair],
        out_specs=pl.BlockSpec((step, lon, half), lambda i: (i, 0, 0)),
        compiler_params=pltpu.CompilerParams(vmem_limit_bytes=48 << 20),
        name="idft",
    )(table, own, above, across_a, across_b, below)


def pack(owner, rank, contrib, owners, first, count):
    blocks, rows, channels = contrib.shape
    out_parts = 8
    out_size = owners // out_parts

    def body(owner_ref, rank_ref, contrib_ref, o_hbm, o_ref, out_sem):
        def step(b, _):
            r = rank_ref[b] - first

            @pl.when((r >= 0) & (r < count))
            def _():
                o_ref[owner_ref[b], r] = contrib_ref[b]

            return 0

        lax.fori_loop(0, blocks, step, 0)
        stores = []
        for i in range(out_parts):
            at = pl.ds(i * out_size, out_size)
            stores.append(pltpu.make_async_copy(o_ref.at[at], o_hbm.at[at], out_sem.at[i]))
            stores[-1].start()
        for c in stores:
            c.wait()

    out = (owners, count, rows, channels)
    return pl.pallas_call(
        body,
        out_shape=pltpu.HBM(out, BF),
        grid_spec=pltpu.PrefetchScalarGridSpec(
            num_scalar_prefetch=2,
            grid=(),
            in_specs=[pl.BlockSpec(memory_space=pltpu.VMEM)],
            out_specs=pl.BlockSpec(memory_space=pl.ANY),
            scratch_shapes=[
                pltpu.VMEM(out, BF),
                pltpu.SemaphoreType.DMA((out_parts,)),
            ],
        ),
        compiler_params=pltpu.CompilerParams(vmem_limit_bytes=48 << 20),
        name="pack",
    )(owner, rank, vmem(contrib))


def add_blocks(i, start, order, target, piece, out, blocks):
    def step(e, _):
        s = order[e]
        rows = pl.ds(pl.multiple_of((target[s] - i * blocks) * BS, BS), BS)
        out[i, rows, :] = out[i, rows, :] + piece[s].astype(F32)
        return 0

    lax.fori_loop(start[i], start[i + 1], step, 0)


def base(core, own, got, lists, piece):
    lat, lon, half = own.shape

    def body(core_ref, start, order, target, own_ref, got_ref, piece_ref, o_ref):
        mine = pl.ds(pl.multiple_of(core_ref[0] * half, half), half)
        other = pl.ds(pl.multiple_of((1 - core_ref[0]) * half, half), half)

        def latitude(i, _):
            o_ref[i, :, mine] = own_ref[i].astype(F32)
            o_ref[i, :, other] = got_ref[i].astype(F32)
            add_blocks(i, start, order, target, piece_ref, o_ref, lon // BS)
            return 0

        lax.fori_loop(0, lat, latitude, 0)

    return pl.pallas_call(
        body,
        out_shape=pltpu.HBM((lat, lon, 2 * half), F32),
        grid_spec=pltpu.PrefetchScalarGridSpec(
            num_scalar_prefetch=4,
            grid=(),
            in_specs=[pl.BlockSpec(memory_space=pltpu.VMEM)] * 3,
            out_specs=pl.BlockSpec(memory_space=pltpu.VMEM),
        ),
        compiler_params=pltpu.CompilerParams(vmem_limit_bytes=48 << 20),
        name="base",
    )(core, *lists, own, got, piece)


def finish(begun, lists, piece):
    lat, lon, channels = begun.shape

    slots = piece.shape[0]
    parts = 6
    size = slots // parts

    def body(start, order, target, begun_hbm, piece_hbm, o_hbm, out, piece_ref, sem, read_sem, piece_sem):
        loads = []
        for j in range(parts):
            at = pl.ds(j * size, size)
            loads.append(pltpu.make_async_copy(piece_hbm.at[at], piece_ref.at[at], piece_sem.at[j]))
            loads[-1].start()

        def read(i):
            return pltpu.make_async_copy(begun_hbm.at[i], out.at[i], read_sem.at[i])

        for i in range(lat):
            read(i).start()
        for c in loads:
            c.wait()

        def write(i):
            return pltpu.make_async_copy(out.at[i], o_hbm.at[i], sem.at[i])

        def latitude(i, _):
            read(i).wait()
            add_blocks(i, start, order, target, piece_ref, out, lon // BS)
            write(i).start()
            return 0

        lax.fori_loop(0, lat, latitude, 0)
        for i in range(lat):
            write(i).wait()

    return pl.pallas_call(
        body,
        out_shape=jax.ShapeDtypeStruct(begun.shape, F32),
        grid_spec=pltpu.PrefetchScalarGridSpec(
            num_scalar_prefetch=3,
            grid=(),
            in_specs=[pl.BlockSpec(memory_space=pl.ANY)] * 2,
            out_specs=pl.BlockSpec(memory_space=pl.ANY),
            scratch_shapes=[
                pltpu.VMEM(begun.shape, F32),
                pltpu.VMEM(piece.shape, BF),
                pltpu.SemaphoreType.DMA((lat,)),
                pltpu.SemaphoreType.DMA((lat,)),
                pltpu.SemaphoreType.DMA((parts,)),
            ],
        ),
        compiler_params=pltpu.CompilerParams(vmem_limit_bytes=48 << 20),
        name="finish",
    )(*lists, begun, piece)


def by_latitude(target, lat, blocks):
    ids = jnp.arange(target.shape[0], dtype=jnp.int32)
    before = (target[None, :] < target[:, None]) | (
        (target[None, :] == target[:, None]) & (ids[None, :] < ids[:, None])
    )
    place = jnp.sum(before.astype(jnp.int32), axis=1)
    order = jnp.sum(jnp.where(place[None, :] == ids[:, None], ids[None, :], 0), axis=1)
    first = jnp.arange(lat + 1, dtype=jnp.int32) * blocks
    start = jnp.sum((target[None, :] < first[:, None]).astype(jnp.int32), axis=1)
    return start, order, target


def shards(
    grid_adjoint_fields,
    interp_weights,
    depart_owner,
    depart_block,
    wave_perm,
    legendre,
    mode_proj,
    mode_back,
    mode_depth,
):
    x = grid_adjoint_fields
    wide = lax.axis_size("wide")
    narrow = lax.axis_size("narrow")
    w = lax.axis_index("wide")
    v = lax.axis_index("narrow")
    y, core = v // 2, v % 2
    ring = narrow // 2
    lat, lon, channels = x.shape
    half = channels // 2
    slots, lat_total, degrees = legendre.shape
    swap = [(i, i ^ 1) for i in range(narrow)]
    up = [(i, (i + 2) % narrow) for i in range(narrow)]
    down = [(i, (i - 2) % narrow) for i in range(narrow)]
    core_ids = core[None].astype(jnp.int32)

    x_give = take_half(1 - core_ids, hbm(x))
    x, x_give = lax.optimization_barrier((x, x_give))
    x_got = lax.ppermute(x_give, "narrow", swap)

    order = wave_perm.reshape(wide, ring, 2, slots).transpose(1, 2, 3, 0)
    order = jnp.concatenate([order, order], axis=0)
    order = jnp.concatenate([order, order[:, :1]], axis=1)
    order = lax.dynamic_slice(order, (y, core, 0, 0), (ring, 2, slots, wide))[:, :, :, None]
    columns = (ring, 2, slots, 2, wide)
    wave = jnp.broadcast_to(order, columns).reshape(-1).astype(F32)
    shift = jnp.tile(jnp.repeat(jnp.array([0.0, 640.0], F32), wide), ring * 2 * slots)
    lons = jnp.arange(2 * lon, dtype=jnp.int32) % lon
    side = jnp.arange(2 * lon, dtype=jnp.int32) // lon
    lons = (lons + lon * jnp.where(side == 0, v, v ^ 1)).astype(F32)

    def table(columns):
        return cosine_of_phase(wave[columns][:, None] * lons[None, :] - shift[columns][:, None])

    def table_t(rows):
        return cosine_of_phase(wave[None, :] * lons[rows][:, None] - shift[None, :])

    blocks = interp_weights.shape[0]
    contrib = jnp.einsum(
        "bai,bac->bic", interp_weights, x.reshape(blocks, BS, channels), preferred_element_type=F32
    ).astype(BF)
    owner = depart_owner[:, 0]
    ids = jnp.arange(blocks, dtype=jnp.int32)
    rank = jnp.sum(
        ((owner[:, None] == owner[None, :]) & (ids[None, :] < ids[:, None])).astype(jnp.int32), axis=1
    )
    slot = owner * CAP + rank
    pick = jnp.arange(wide * CAP, dtype=jnp.int32)[:, None] == slot[None, :]
    target = jnp.max(jnp.where(pick, depart_block[None, :], -1), axis=1)
    cut = [0]
    for n in COUNTS:
        cut.append(cut[-1] + n)

    def send_deposit(piece):
        out = lax.all_to_all(
            piece.reshape(wide, -1, channels), "wide", split_axis=0, concat_axis=0, tiled=True
        )
        return out.reshape(-1, BS, channels)

    piece_1 = pack(owner, rank, contrib, wide, cut[0], COUNTS[0])
    got_1 = send_deposit(piece_1)

    per = 256
    x_late, piece_1 = lax.optimization_barrier((x, piece_1))
    x = x_late
    far_a, far_b = dft(core_ids, table(slice(2 * per, 3 * per)), x, x_got, 4)

    near = jnp.concatenate([wave[3 * per :], wave[: 2 * per]])
    near_shift = jnp.concatenate([shift[3 * per :], shift[: 2 * per]])
    near = cosine_of_phase(near[:, None] * lons[None, :] - near_shift[:, None])
    down_a, down_b, own_a, own_b, up_a, up_b = dft(core_ids, near, x, x_got, 4)

    relay_a = lax.ppermute(far_a, "narrow", up)
    relay_b = lax.ppermute(far_b, "narrow", down)
    direct_b = lax.ppermute(up_b, "narrow", up)
    direct_a = lax.ppermute(down_a, "narrow", down)
    sum_a = lax.ppermute((relay_a.astype(F32) + up_a.astype(F32)).astype(BF), "narrow", up)
    sum_b = lax.ppermute((relay_b.astype(F32) + down_b.astype(F32)).astype(BF), "narrow", down)
    marks = jnp.pad(
        target.reshape(wide, 1, CAP).astype(BF), ((0, 0), (0, lat - 1), (0, 128 - CAP))
    )
    slot_waves = lax.dynamic_slice(wave_perm, ((w * narrow + v) * slots,), (slots,))
    mode_ids = jnp.concatenate([core_ids, slot_waves])
    proj, back = mode_proj.astype(BF), mode_back.astype(BF)
    piece_2 = pack(owner, rank, contrib, wide, cut[1], COUNTS[1])
    own_a, piece_2, proj, back, marks = lax.optimization_barrier(
        (own_a, piece_2, proj, back, marks)
    )
    rows, other = to_rows([own_a, sum_a, direct_a, own_b, sum_b, direct_b], marks, wide)
    rows = join(rows, vmem(lax.ppermute(other, "narrow", swap)))
    rows, got_1 = lax.optimization_barrier((rows, got_1))
    rows = lax.all_to_all(rows, "wide", split_axis=0, concat_axis=0, tiled=True)
    targets = rows[:, 0, 4 * channels : 4 * channels + CAP].astype(jnp.int32)
    lists = [
        by_latitude(targets[:, i:j].reshape(-1), lat, lon // BS) for i, j in zip(cut, cut[1:])
    ]
    synth = modes(
        mode_ids, rows.reshape(lat_total, -1), hbm(legendre), vmem(proj), vmem(back),
        mode_depth.reshape(1, -1), wide, lat,
    )
    synth = lax.all_to_all(synth, "wide", split_axis=0, concat_axis=0, tiled=True)
    piece_2, synth = lax.optimization_barrier((piece_2, synth))
    got_2 = send_deposit(piece_2)

    own = to_columns(synth, lax.ppermute(synth[:, 1], "narrow", swap))
    below = lax.ppermute(own, "narrow", up)
    above = lax.ppermute(own, "narrow", down)
    across_a = lax.ppermute(below[0], "narrow", up)
    across_b = lax.ppermute(above[1], "narrow", down)
    pieces = [own, above, across_a, across_b, below]
    wave_got = lax.ppermute(idft(table_t(slice(lon, 2 * lon)), *pieces, 4), "narrow", swap)
    wave_own = idft(table_t(slice(0, lon)), *pieces, 4)
    begun = base(core_ids, wave_own, wave_got, lists[0], got_1)
    return finish(hbm(begun), lists[1], hbm(got_2))


def solution(mesh):
    in_specs = (
        P("wide", "narrow", None),
        P(("wide", "narrow"), None, None),
        P(("wide", "narrow"), None),
        P(("wide", "narrow")),
        P(),
        P(("wide", "narrow"), None, None),
        P(),
        P(),
        P(),
    )
    out_specs = P("wide", "narrow", None)
    return jax.shard_map(shards, mesh=mesh, in_specs=in_specs, out_specs=out_specs, check_vma=False)
```
